512 devices in a mesh: wide: 128 (over y, z, core), narrow: 4 (over x).
Axes of the slice: x: 4, y: 8, z: 8, core: 2. Of those that a mesh axis runs over, the one named last changes fastest.
Arguments:
- initial_heat_level: float32 [512, 256, 256], P('narrow', 'wide'), may hold values from -4 to 6.5
- heat_transmission: float32 [512, 256, 256], P('narrow', 'wide'), may hold values from 1 to 10
Outputs:
- next_temperature: float32 [512, 256, 256], P('narrow', 'wide')
The draws below stay inside these ranges and needn't reach their ends.
All inputs are finite; a program needn't handle non-finite values.
Results may differ from the reference program's by a relative error of at most 0.0014.
Values sent between devices are 32-bit elements; how exact they have to be, the bound alone decides.
A program may use at most 128 MiB of HBM per device.

```python
import math
import jax
import jax.numpy as jnp
from jax import lax

N_LINE = 256
NZ = 512


def draw_initial_heat_level(key, part):
    rough = jax.random.normal(key, (NZ, N_LINE, N_LINE), jnp.float32)
    return jnp.clip(rough, -4.0, 6.5)


def level_of(key, shape, pieces, smallest, high):
    gain, own = 1.0, jax.random.fold_in(key, 6)
    for axis_at, parts in pieces:
        heights = jnp.exp(jax.random.uniform(jax.random.fold_in(own, axis_at), (parts,), jnp.float32, smallest / len(pieces), high / len(pieces)))
        gain = gain * jnp.repeat(heights, shape[axis_at] // parts).reshape([-1 if axis == axis_at else 1 for axis in range(len(shape))])
    return gain


def setup_inputs(seed: int = 0) -> dict:
    seeds = jax.random.split(jax.random.key(seed), 3)
    return {
        "initial_heat_level": draw_initial_heat_level(jax.random.fold_in(seeds[2], 71), 0),
        "heat_transmission": jnp.clip(jnp.exp(math.log(10.0) - 2.3025851 * jax.random.uniform(seeds[1], (NZ, N_LINE, N_LINE), jnp.float32) ** level_of(seeds[1], (NZ, N_LINE, N_LINE), ((0, 4), (1, 128)), -0.2, 0.2)), 1.0, 10.0),
    }


MIDPOINT_WEIGHT = 250.0
FULL_TIME_WEIGHT = 500.0

def face_pair(cond_field, along):
    extent = cond_field.shape[along]
    lower_cells = lax.slice_in_dim(cond_field, 0, extent - 1, axis=along)
    upper_cells = lax.slice_in_dim(cond_field, 1, extent, axis=along)
    between = 2.0 * lower_cells * upper_cells / (lower_cells + upper_cells)
    zero_face = jnp.zeros_like(lax.slice_in_dim(cond_field, 0, 1, axis=along))
    return (jnp.concatenate([zero_face, between], along), jnp.concatenate([between, zero_face], along))

def directional_laplacian(field_data, lower_face, upper_face, along):
    extent = field_data.shape[along]
    zero_face = jnp.zeros_like(lax.slice_in_dim(field_data, 0, 1, axis=along))
    previous = jnp.concatenate([zero_face, lax.slice_in_dim(field_data, 0, extent - 1, axis=along)], along)
    following = jnp.concatenate([lax.slice_in_dim(field_data, 1, extent, axis=along), zero_face], along)
    return upper_face * (following - field_data) - lower_face * (field_data - previous)

def solve_along(right_side, lower_face, upper_face, along):
    moved_rhs = jnp.moveaxis(right_side, along, -1)
    moved_low = jnp.moveaxis(lower_face, along, -1)
    moved_up = jnp.moveaxis(upper_face, along, -1)
    sub_diag = -MIDPOINT_WEIGHT * moved_low
    main_diag = 1.0 + MIDPOINT_WEIGHT * (moved_low + moved_up)
    super_diag = -MIDPOINT_WEIGHT * moved_up
    solution = lax.linalg.tridiagonal_solve(sub_diag, main_diag, super_diag, moved_rhs[..., None])[..., 0]
    return jnp.moveaxis(solution, -1, along)

def reference(initial_heat_level, heat_transmission):
    width_inflow_below, width_inflow_above = face_pair(heat_transmission, 2)
    depth_inflow_below, depth_inflow_above = face_pair(heat_transmission, 1)
    height_inflow_below, height_inflow_above = face_pair(heat_transmission, 0)
    width_spread_term = directional_laplacian(initial_heat_level, width_inflow_below, width_inflow_above, 2)
    depth_spread_term = directional_laplacian(initial_heat_level, depth_inflow_below, depth_inflow_above, 1)
    height_spread_term = directional_laplacian(initial_heat_level, height_inflow_below, height_inflow_above, 0)
    width_system_source = initial_heat_level + MIDPOINT_WEIGHT * width_spread_term + FULL_TIME_WEIGHT * depth_spread_term + FULL_TIME_WEIGHT * height_spread_term
    after_x = solve_along(width_system_source, width_inflow_below, width_inflow_above, 2)
    after_y = solve_along(after_x - MIDPOINT_WEIGHT * depth_spread_term, depth_inflow_below, depth_inflow_above, 1)
    return solve_along(after_y - MIDPOINT_WEIGHT * height_spread_term, height_inflow_below, height_inflow_above, 0)
```

```python
import functools

import jax
import jax.numpy as jnp
from jax import lax
from jax.experimental import pallas as pl
from jax.experimental.pallas import tpu as pltpu
from jax.sharding import PartitionSpec as P

MESH = pl.DeviceIdType.MESH
WIDE, RING, PLANES, X = 128, 8, 128, 256
PAD = 8
TX, TZ = 32, 16
FACE = 500.0


def face(lower, upper):
    return FACE * lower * upper / (lower + upper)


def forward_matrix(masses, sub, closing):
    p, h = masses[0], sub[0]
    ratios, inverses, reach, sigma = [], [], [], None
    for t in range(1, len(sub)):
        inv = 1.0 / (p + h + sub[t])
        hm = h * inv
        sigma = hm * p if sigma is None else sigma + hm * p
        r = sub[t] * inv
        ratios.append(r)
        inverses.append(inv)
        reach.append(hm)
        p = masses[t] + r * p
        h = r * h
    return p, h, sigma, ratios, inverses, reach


def neighbours(value, step):
    size = value.shape[0]
    return pltpu.roll(value, step, 0), pltpu.roll(value, size - step, 0)


def spread_factor(mass, low):
    high = pltpu.roll(low, 7, 0)
    levels = []
    for step in (1, 2, 4):
        inv = 1.0 / (mass + low + high)
        inv_down, inv_up = neighbours(inv, step)
        alpha, gamma = low * inv_down, high * inv_up
        mass_down, mass_up = neighbours(mass, step)
        mass = mass + alpha * mass_down + gamma * mass_up
        low = alpha * pltpu.roll(low, step, 0)
        high = gamma * pltpu.roll(high, 8 - step, 0)
        levels.append((alpha, gamma))
    return levels, 1.0 / mass


def spread_solve(levels, inverse, value):
    for (alpha, gamma), step in zip(levels, (1, 2, 4)):
        down, up = neighbours(value, step)
        value = value + alpha * down + gamma * up
    return value * inverse


def kernel(u_in, k_in, out, un, kn, az, uprev, unext, kprev, knext, ay,
           work, xr, xi, xh, xg, xa, zr, zi, zh, zg,
           a_mine, a_other, d_mine, d_other, ym_r, ym_i, ym_h, y_g,
           zm_out, zm_in, zr_out, zr_in, l_r, l_i, l_h, l_g,
           yk_out, yk_in, yr_out, yr_in, sol8, back_out, back_in, back_core, home_core,
           nm_out, nm_in, nr_out, nr_in, edge_in, xlev, zlev,
           s_halo, r_halo, s_edge, r_edge, s_core, r_core, s_ring, r_ring, s_col, r_col, s_n, r_n):
    w = lax.axis_index("wide")
    n = lax.axis_index("narrow")
    core = lax.rem(w, 2)
    zc = lax.rem(w // 2, RING)
    yc = w // (2 * RING)
    partner = {"wide": w + 1 - 2 * core}
    upper_dev = {"wide": lax.rem(w + 1, WIDE)}
    lower_dev = {"wide": lax.rem(w + WIDE - 1, WIDE)}

    def ring_dev(i):
        return {"wide": yc * (2 * RING) + lax.rem(zc + i, RING) * 2 + core}

    def col_dev(i):
        return {"wide": lax.rem(yc + i, RING) * (2 * RING) + zc * 2 + core}

    def n_dev(i):
        return {"narrow": lax.rem(n + i, 4)}

    def copy(src, dst, send, recv, dev):
        return pltpu.make_async_remote_copy(
            src_ref=src, dst_ref=dst, send_sem=send, recv_sem=recv,
            device_id=dev, device_id_type=MESH)

    barrier = pltpu.get_barrier_semaphore()
    for dev in ([upper_dev, lower_dev] + [ring_dev(i) for i in range(1, 8)]
                + [col_dev(i) for i in range(1, 8)] + [n_dev(i) for i in range(1, 4)]):
        pl.semaphore_signal(barrier, 1, device_id=dev, device_id_type=MESH)

    rows = pl.ds(PAD, PLANES)
    for j in range(2):
        for xt in range(2):
            grab = pl.ds(xt * 2 + j, PLANES, stride=4)
            kn[j * 2 + xt, rows] = k_in[grab, :]
            un[j * 2 + xt, rows] = u_in[grab, :]
    row0, row1 = pl.ds(0, 2), pl.ds(2, 2)

    pl.semaphore_wait(barrier, 19)
    pending = []

    def go(src, dst, send, recv, dev):
        c = copy(src, dst, send, recv, dev)
        c.start()
        pending.append(c)
        return c

    k_halo = [go(kn.at[row1, rows], kprev, s_halo.at[0], r_halo.at[0], upper_dev),
              go(kn.at[row0, rows], knext, s_halo.at[1], r_halo.at[1], lower_dev)]
    top, bottom = pl.ds(PAD + PLANES - 8, 8), pl.ds(PAD, 8)
    edge = [go(kn.at[:, top], edge_in.at[0], s_edge.at[0], r_edge.at[0], n_dev(1)),
            go(kn.at[:, bottom], edge_in.at[1], s_edge.at[1], r_edge.at[1], n_dev(3)),
            go(un.at[:, top], edge_in.at[2], s_edge.at[2], r_edge.at[2], n_dev(1)),
            go(un.at[:, bottom], edge_in.at[3], s_edge.at[3], r_edge.at[3], n_dev(3))]
    u_halo = [go(un.at[row1, rows], uprev, s_halo.at[2], r_halo.at[2], upper_dev),
              go(un.at[row0, rows], unext, s_halo.at[3], r_halo.at[3], lower_dev)]

    sub8 = lax.broadcasted_iota(jnp.int32, (8, 1), 0)
    first = sub8 == 0

    def to_x(src):
        for j in range(2):
            for xt in range(2):
                work[j, pl.ds(xt * 128, 128)] = src[j * 2 + xt, rows].T

    to_x(kn)

    def xrow(ref, t):
        return jnp.concatenate(
            [ref[c, pl.ds(t, 8, stride=TX), :] for c in range(2)], axis=1)

    k_before = pltpu.roll(xrow(work, TX - 1), 1, 0)
    p = h = sigma = None
    for t in range(TX):
        k_now = xrow(work, t)
        a = face(k_before, k_now)
        k_before = k_now
        if t == 0:
            a = jnp.where(first, 0.0, a)
            p, h = jnp.ones_like(a), a
        else:
            inv = 1.0 / (p + h + a)
            hm = h * inv
            sigma = hm * p if sigma is None else sigma + hm * p
            r = a * inv
            xr[t] = r
            xi[t - 1] = inv
            xh[t - 1] = hm
            p = 1.0 + r * p
            h = r * h
    x_levels, x_inv = spread_factor(p + jnp.where(sub8 == 7, 0.0, pltpu.roll(sigma, 7, 0)), h)
    for i, (alpha, gamma) in enumerate(x_levels):
        xlev[2 * i] = alpha
        xlev[2 * i + 1] = gamma
    xlev[6] = x_inv

    for c in edge:
        c.wait_recv()
    kn[:, pl.ds(0, PAD)] = edge_in[0]
    kn[:, pl.ds(PAD + PLANES, PAD)] = edge_in[1]
    un[:, pl.ds(0, PAD)] = edge_in[2]
    un[:, pl.ds(PAD + PLANES, PAD)] = edge_in[3]
    for q in range(9):
        size = 8 if q == 8 else 16
        low = kn[:, pl.ds(PAD - 1 + q * 16, size)]
        high = kn[:, pl.ds(PAD + q * 16, size)]
        value = face(low, high)
        if q in (0, 8):
            at = lax.broadcasted_iota(jnp.int32, (size, 1), 0)
            value = jnp.where((at == 0) & (n == (0 if q == 0 else 3)), 0.0, value)
        az[:, pl.ds(PAD + q * 16, size)] = value

    for c in k_halo:
        c.wait_recv()
    for q in range(8):
        part, src = pl.ds(q * 16, 16), pl.ds(PAD + q * 16, 16)
        k0, k1 = kn[row0, src], kn[row1, src]
        ay[0, :, part] = jnp.where(w > 0, face(kprev[:, part], k0), 0.0)
        ay[1, :, part] = face(k0, k1)
        ay[2, :, part] = jnp.where(w < WIDE - 1, face(k1, knext[:, part]), 0.0)
    mine = pl.multiple_of(core * 64, 64)
    other = pl.multiple_of(64 - core * 64, 64)
    a_core = go(ay.at[pl.ds(0, 2), :, pl.ds(other, 64)], a_other, s_core.at[0], r_core.at[0], partner)

    for c in u_halo:
        c.wait_recv()
    for q in range(8):
        part, src = pl.ds(q * 16, 16), pl.ds(PAD + q * 16, 16)
        u0, u1 = un[row0, src], un[row1, src]
        mid = ay[1, :, part] * (u1 - u0)
        ly = (mid - ay[0, :, part] * (u0 - uprev[:, part]),
              ay[2, :, part] * (unext[:, part] - u1) - mid)
        for j, (row, u) in enumerate(((row0, u0), (row1, u1))):
            up, down = pl.ds(PAD + q * 16 + 1, 16), pl.ds(PAD + q * 16 - 1, 16)
            lz = az[row, up] * (un[row, up] - u) - az[row, src] * (u - un[row, down])
            zg[row, part] = u + ly[j] + lz
    for j in range(2):
        for xt in range(2):
            work[j, pl.ds(xt * 128, 128)] = zg[j * 2 + xt].T
    g = acc = None
    for t in range(TX):
        f = xrow(work, t)
        g = f if t == 0 else f + xr[t] * g
        if t < TX - 1:
            acc = xh[t] * g if acc is None else acc + xh[t] * g
            xg[t] = g * xi[t]
    g = g + jnp.where(sub8 == 7, 0.0, pltpu.roll(acc, 7, 0))
    sep = spread_solve([(xlev[2 * i], xlev[2 * i + 1]) for i in range(3)], xlev[6], g)
    left = jnp.where(first, 0.0, pltpu.roll(sep, 1, 0))
    value = sep
    for t in range(TX - 1, -1, -1):
        if t < TX - 1:
            value = xg[t] + xh[t] * left + xr[t + 1] * value
        for c in range(2):
            work[c, pl.ds(t, 8, stride=TX), :] = value[:, c * 128:(c + 1) * 128]
    for j in range(2):
        for xt in range(2):
            back = work[j, pl.ds(xt * 128, 128)].T
            xa[j, xt] = 2.0 * (back - un[j * 2 + xt, rows])
    d_core = go(xa.at[:, :, pl.ds(other, 64)], d_other, s_core.at[1], r_core.at[1], partner)

    a_core.wait_recv()
    swap = core == 1
    a_mine[...] = ay[pl.ds(0, 2), :, pl.ds(mine, 64)]
    for o in range(8):
        part = pl.ds(o * 8, 8)
        own, far = [a_mine[j, :, part] for j in range(2)], [a_other[j, :, part] for j in range(2)]
        sub = ([jnp.where(swap, far[j], own[j]) for j in range(2)]
               + [jnp.where(swap, own[j], far[j]) for j in range(2)])
        one = jnp.ones_like(sub[0])
        p, h, sigma, ratios, inverses, reach = forward_matrix([one] * 4, sub, None)
        zm_out[o, 0], zm_out[o, 1], zm_out[o, 2] = p, sigma, h
        for t in range(3):
            ym_r[o, t], ym_i[o, t], ym_h[o, t] = ratios[t], inverses[t], reach[t]
    zm_in[zc] = zm_out[zc]
    zm = [go(zm_out.at[lax.rem(zc + i, RING)], zm_in.at[zc], s_ring.at[0, i], r_ring.at[0, i],
             ring_dev(i)) for i in range(1, 8)]

    d_core.wait_recv()
    d_mine[...] = xa[:, :, pl.ds(mine, 64)]
    for o in range(8):
        part = pl.ds(o * 8, 8)
        own, far = [d_mine[j, :, part] for j in range(2)], [d_other[j, :, part] for j in range(2)]
        f = ([jnp.where(swap, far[j], own[j]) for j in range(2)]
             + [jnp.where(swap, own[j], far[j]) for j in range(2)])
        g, acc = f[0], None
        for t in range(3):
            y_g[o, t] = g * ym_i[o, t]
            add = ym_h[o, t] * g
            acc = add if acc is None else acc + add
            g = f[t + 1] + ym_r[o, t] * g
        zr_out[o, 0], zr_out[o, 1] = g, acc
    zr_in[zc] = zr_out[zc]
    zrc = [go(zr_out.at[lax.rem(zc + i, RING)], zr_in.at[zc], s_ring.at[1, i], r_ring.at[1, i],
              ring_dev(i)) for i in range(1, 8)]

    for c in zm:
        c.wait_recv()
    masses = [zm_in[s, 0] + zm_in[s + 1, 1] for s in range(7)] + [zm_in[7, 0]]
    p, h, sigma, ratios, inverses, reach = forward_matrix(
        masses, [zm_in[s, 2] for s in range(8)], None)
    yk_out[0], yk_out[1], yk_out[2] = p, zm_in[0, 1] + sigma, h
    for t in range(7):
        l_r[t], l_i[t], l_h[t] = ratios[t], inverses[t], reach[t]
    yk_in[yc] = yk_out[...]
    yk = [go(yk_out, yk_in.at[yc], s_col.at[0, i], r_col.at[0, i], col_dev(i)) for i in range(1, 8)]

    p = h = sigma = None
    def zrow(ref, t):
        return jnp.concatenate([ref[c, pl.ds(t, 8, stride=TZ), :] for c in range(4)], axis=1)

    for t in range(TZ):
        a = zrow(az, PAD + t)
        if t == 0:
            p, h = jnp.ones_like(a), a
        else:
            inv = 1.0 / (p + h + a)
            hm = h * inv
            sigma = hm * p if sigma is None else sigma + hm * p
            r = a * inv
            zr[t] = r
            zi[t - 1] = inv
            zh[t - 1] = hm
            p = 1.0 + r * p
            h = r * h
    last = sub8 == 7
    mass = p + jnp.where(last, 0.0, pltpu.roll(sigma, 7, 0))
    h_up = pltpu.roll(h, 7, 0)
    low = jnp.where(first | last, 0.0, h)
    ground = mass + jnp.where(first, h, 0.0) + jnp.where(sub8 == 6, h_up, 0.0)
    levels, inverse = spread_factor(jnp.where(last, 1.0, ground), low)
    for i, (alpha, gamma) in enumerate(levels):
        zlev[2 * i] = alpha
        zlev[2 * i + 1] = gamma
    zlev[6] = inverse
    from_low = spread_solve(levels, inverse, jnp.where(first, h, 0.0))
    from_high = spread_solve(levels, inverse, jnp.where(sub8 == 6, h_up, 0.0))
    own_mass = spread_solve(levels, inverse, jnp.where(last, 0.0, mass))
    zlev[7] = from_low
    zlev[8] = from_high
    zlev[9] = h

    def pick(value, s):
        return jnp.broadcast_to(value[s:s + 1], value.shape)

    h0, h7 = pick(h, 0), pick(h, 7)
    nm_out[0] = pick(mass, 7) + h7 * pick(own_mass, 6)
    nm_out[1] = pick(sigma, 0) + h0 * pick(own_mass, 0)
    nm_out[2] = h0 * pick(from_high, 0)
    nm = [go(nm_out, nm_in.at[pl.ds(3 * (i - 1), 3)], s_n.at[0, i], r_n.at[0, i], n_dev(i))
          for i in range(1, 4)]

    for c in zrc:
        c.wait_recv()
    g, acc = zr_in[0, 0] + zr_in[1, 1], None
    for s in range(7):
        l_g[s] = g * l_i[s]
        add = l_h[s] * g
        acc = add if acc is None else acc + add
        g = zr_in[s + 1, 0] + l_r[s] * g
        if s < 6:
            g = g + zr_in[s + 2, 1]
    yr_out[0], yr_out[1] = g, zr_in[0, 1] + acc
    yr_in[yc] = yr_out[...]
    yr = [go(yr_out, yr_in.at[yc], s_col.at[1, i], r_col.at[1, i], col_dev(i)) for i in range(1, 8)]

    for c in yk:
        c.wait_recv()
    masses = [yk_in[s, 0] + yk_in[s + 1, 1] for s in range(7)] + [yk_in[7, 0]]
    sub = [yk_in[s, 2] for s in range(8)]
    p, ratios, inverses = masses[0], [], []
    for s in range(1, 8):
        inv = 1.0 / (p + sub[s])
        ratios.append(sub[s] * inv)
        inverses.append(inv)
        p = masses[s] + ratios[-1] * p
    inverses.append(1.0 / p)
    for c in yr:
        c.wait_recv()
    values = [yr_in[0, 0] + yr_in[1, 1]]
    for s in range(1, 8):
        g = yr_in[s, 0] + ratios[s - 1] * values[-1]
        values.append(g + yr_in[s + 1, 1] if s < 7 else g)
    value = values[7] * inverses[7]
    sol8[8] = value
    for s in range(6, -1, -1):
        value = values[s] * inverses[s] + ratios[s] * value
        sol8[s + 1] = value
    sol8[0] = jnp.zeros_like(value)
    left, value = sol8[yc], sol8[yc + 1]
    back_out[7, 1] = value
    for s in range(6, -1, -1):
        value = l_g[s] + l_h[s] * left + l_r[s] * value
        back_out[s, 1] = value
        back_out[s + 1, 0] = value
    back_out[0, 0] = left
    back_in[zc] = back_out[zc]
    bk = [go(back_out.at[lax.rem(zc + i, RING)], back_in.at[zc], s_ring.at[2, i], r_ring.at[2, i],
             ring_dev(i)) for i in range(1, 8)]
    for c in bk:
        c.wait_recv()
    for o in range(8):
        part = pl.ds(o * 8, 8)
        left, value = back_in[o, 0], back_in[o, 1]
        solved = [None, None, None, value]
        for t in range(2, -1, -1):
            value = y_g[o, t] + ym_h[o, t] * left + ym_r[o, t] * value
            solved[t] = value
        for j in range(2):
            back_core[j, :, part] = jnp.where(swap, solved[j], solved[2 + j])
            d_mine[j, :, part] = jnp.where(swap, solved[2 + j], solved[j])
    home = go(back_core, home_core, s_core.at[2], r_core.at[2], partner)
    for j in range(2):
        zg[pl.ds(2 * j, 2), pl.ds(mine, 64)] = d_mine[j]
    home.wait_recv()
    for j in range(2):
        zg[pl.ds(2 * j, 2), pl.ds(other, 64)] = home_core[j]

    g = acc = None
    for t in range(TZ):
        f = zrow(zg, t)
        g = f if t == 0 else f + zr[t] * g
        if t < TZ - 1:
            acc = zh[t] * g if acc is None else acc + zh[t] * g
            zi[t] = g * zi[t]
    g = g + jnp.where(last, 0.0, pltpu.roll(acc, 7, 0))
    levels = [(zlev[2 * i], zlev[2 * i + 1]) for i in range(3)]
    base = spread_solve(levels, zlev[6], jnp.where(last, 0.0, g))
    h = zlev[9]
    nr_out[0] = pick(g, 7) + pick(h, 7) * pick(base, 6)
    nr_out[1] = pick(acc, 0) + pick(h, 0) * pick(base, 0)
    nr = [go(nr_out, nr_in.at[pl.ds(2 * (i - 1), 2)], s_n.at[1, i], r_n.at[1, i], n_dev(i))
          for i in range(1, 4)]
    for c in nm:
        c.wait_recv()

    def stacked(own, ref, offset, step):
        whole = jnp.where(sub8 == n, own, 0.0)
        for i in range(1, 4):
            whole = jnp.where(sub8 == lax.rem(n + 4 - i, 4), ref[offset + step * (i - 1)], whole)
        return whole

    top_mass, low_mass, coupling = [stacked(nm_out[v], nm_in, v, 3) for v in range(3)]
    high = pltpu.roll(coupling, 7, 0)
    mass = top_mass + jnp.where(sub8 < 3, pltpu.roll(low_mass, 7, 0), 0.0)
    mass = jnp.where(sub8 < 4, mass, 1.0)
    n_levels, n_inverse = spread_factor(mass, coupling)
    for c in nr:
        c.wait_recv()
    top_rhs, low_rhs = [stacked(nr_out[v], nr_in, v, 2) for v in range(2)]
    rhs = top_rhs + jnp.where(sub8 < 3, pltpu.roll(low_rhs, 7, 0), 0.0)
    ends = spread_solve(n_levels, n_inverse, rhs)
    mine_end = jnp.sum(jnp.where(sub8 == n, ends, 0.0), axis=0, keepdims=True)
    left_end = jnp.sum(jnp.where(sub8 == n - 1, ends, 0.0), axis=0, keepdims=True)
    sep = jnp.where(last, mine_end, base + zlev[7] * left_end + zlev[8] * mine_end)
    left = jnp.where(first, left_end, pltpu.roll(sep, 1, 0))
    value = sep
    for t in range(TZ - 1, -1, -1):
        if t < TZ - 1:
            value = zi[t] + zh[t] * left + zr[t + 1] * value
        for c in range(4):
            zg[c, pl.ds(t, 8, stride=TZ), :] = value[:, c * 128:(c + 1) * 128]
    for j in range(2):
        for xt in range(2):
            c = j * 2 + xt
            out[pl.ds(xt * 2 + j, PLANES, stride=4), :] = un[c, rows] + zg[c]
    for c in pending:
        c.wait_send()


def flat(value):
    return value.reshape(PLANES, 2, 2, 128).transpose(0, 2, 1, 3).reshape(4 * PLANES, 128)


def per_device(initial_heat_level, heat_transmission):
    f32 = jnp.float32
    V = lambda *shape: pltpu.VMEM(shape, f32)
    S = lambda *shape: pltpu.SemaphoreType.DMA(shape)
    natural = (4, PLANES + 2 * PAD, 128)
    halo = (2, PLANES, 128)
    half = (2, 2, 64, 128)
    tile = (2, 8, 128)
    scratch = [
        V(*natural), V(*natural), V(*natural),
        V(*halo), V(*halo), V(*halo), V(*halo), V(3, *halo),
        V(2, X, 128), V(TX, 8, 256), V(TX, 8, 256), V(TX, 8, 256), V(TX, 8, 256), V(2, *halo),
        V(TZ, 8, 512), V(TZ, 8, 512), V(TZ, 8, 512), V(4, PLANES, 128),
        V(*half), V(*half), V(*half), V(*half),
        V(8, 3, *tile), V(8, 3, *tile), V(8, 3, *tile), V(8, 3, *tile),
        V(8, 3, *tile), V(8, 3, *tile), V(8, 2, *tile), V(8, 2, *tile),
        V(7, *tile), V(7, *tile), V(7, *tile), V(7, *tile),
        V(3, *tile), V(8, 3, *tile), V(2, *tile), V(8, 2, *tile), V(9, *tile),
        V(8, 2, *tile), V(8, 2, *tile), V(*half), V(*half),
        V(3, 8, 512), V(9, 8, 512), V(2, 8, 512), V(6, 8, 512), V(4, 4, 8, 128),
        V(7, 8, 256), V(10, 8, 512),
        S(4), S(4), S(4), S(4), S(3), S(3), S(3, 8), S(3, 8), S(2, 8), S(2, 8), S(2, 4), S(2, 4),
    ]
    vmem = pl.BlockSpec(memory_space=pltpu.VMEM)
    result = pl.pallas_call(
        kernel,
        out_shape=jax.ShapeDtypeStruct((4 * PLANES, 128), f32),
        in_specs=[vmem, vmem],
        out_specs=vmem,
        scratch_shapes=scratch,
        compiler_params=pltpu.CompilerParams(
            collective_id=0, has_side_effects=True, vmem_limit_bytes=40 << 20),
    )(flat(initial_heat_level), flat(heat_transmission))
    return result.reshape(PLANES, 2, 2, 128).transpose(0, 2, 1, 3).reshape(PLANES, 2, X)


def solution(mesh):
    spec = P("narrow", "wide", None)
    return jax.shard_map(
        per_device, mesh=mesh, in_specs=(spec, spec), out_specs=spec, check_vma=False)
```

```python
import functools

import jax
import jax.numpy as jnp
from jax import lax
from jax.experimental import pallas as pl
from jax.experimental.pallas import tpu as pltpu
from jax.sharding import PartitionSpec as P

MESH = pl.DeviceIdType.MESH
WIDE, RING, PLANES, X = 128, 8, 128, 256
PAD = 8
TX, TZ = 32, 16
FACE = 500.0
FAR = (4, 3, 5, 2, 6, 1, 7)


def face(lower, upper):
    return FACE * lower * upper / (lower + upper)


def forward_matrix(masses, sub, closing):
    p, h = masses[0], sub[0]
    ratios, inverses, reach, sigma = [], [], [], None
    for t in range(1, len(sub)):
        inv = 1.0 / (p + h + sub[t])
        hm = h * inv
        sigma = hm * p if sigma is None else sigma + hm * p
        r = sub[t] * inv
        ratios.append(r)
        inverses.append(inv)
        reach.append(hm)
        p = masses[t] + r * p
        h = r * h
    return p, h, sigma, ratios, inverses, reach


def neighbours(value, step):
    size = value.shape[0]
    return pltpu.roll(value, step, 0), pltpu.roll(value, size - step, 0)


def spread_factor(mass, low):
    high = pltpu.roll(low, 7, 0)
    levels = []
    for step in (1, 2, 4):
        inv = 1.0 / (mass + low + high)
        inv_down, inv_up = neighbours(inv, step)
        alpha, gamma = low * inv_down, high * inv_up
        mass_down, mass_up = neighbours(mass, step)
        mass = mass + alpha * mass_down + gamma * mass_up
        low = alpha * pltpu.roll(low, step, 0)
        high = gamma * pltpu.roll(high, 8 - step, 0)
        levels.append((alpha, gamma))
    return levels, 1.0 / mass


def spread_solve(levels, inverse, value):
    for (alpha, gamma), step in zip(levels, (1, 2, 4)):
        down, up = neighbours(value, step)
        value = value + alpha * down + gamma * up
    return value * inverse


def kernel(u_hbm, k_hbm, out, u_in, k_in, s_load, un, kn, az, uprev, unext, kprev, knext, ay,
           work, xr, xi, xh, xg, xa, zr, zi, zh, zg,
           a_mine, a_other, d_mine, d_other, ym_r, ym_i, ym_h, y_g,
           zm_out, zm_in, zr_out, zr_in, l_r, l_i, l_h, l_g,
           yk_out, yk_in, yr_out, yr_in, sol8, back_out, back_in, back_core, home_core,
           nm_out, nm_in, nr_out, nr_in, edge_in, xlev, zlev,
           s_halo, r_halo, s_edge, r_edge, s_core, r_core, s_ring, r_ring, s_col, r_col, s_n, r_n):
    w = lax.axis_index("wide")
    n = lax.axis_index("narrow")
    core = lax.rem(w, 2)
    zc = lax.rem(w // 2, RING)
    yc = w // (2 * RING)
    partner = {"wide": w + 1 - 2 * core}
    upper_dev = {"wide": lax.rem(w + 1, WIDE)}
    lower_dev = {"wide": lax.rem(w + WIDE - 1, WIDE)}

    def ring_dev(i):
        return {"wide": yc * (2 * RING) + lax.rem(zc + i, RING) * 2 + core}

    def col_dev(i):
        return {"wide": lax.rem(yc + i, RING) * (2 * RING) + zc * 2 + core}

    def n_dev(i):
        return {"narrow": lax.rem(n + i, 4)}

    def copy(src, dst, send, recv, dev):
        return pltpu.make_async_remote_copy(
            src_ref=src, dst_ref=dst, send_sem=send, recv_sem=recv,
            device_id=dev, device_id_type=MESH)

    loads = [pltpu.make_async_copy(k_hbm, k_in, s_load.at[0]),
             pltpu.make_async_copy(u_hbm, u_in, s_load.at[1])]
    for c in loads:
        c.start()
    barrier = pltpu.get_barrier_semaphore()
    for dev in ([upper_dev, lower_dev] + [ring_dev(i) for i in range(1, 8)]
                + [col_dev(i) for i in range(1, 8)] + [n_dev(i) for i in range(1, 4)]):
        pl.semaphore_signal(barrier, 1, device_id=dev, device_id_type=MESH)

    rows = pl.ds(PAD, PLANES)
    for c, src, dst in zip(loads, (k_in, u_in), (kn, un)):
        c.wait()
        for j in range(2):
            for xt in range(2):
                dst[j * 2 + xt, rows] = src[pl.ds(xt * 2 + j, PLANES, stride=4), :]
    row0, row1 = pl.ds(0, 2), pl.ds(2, 2)

    pl.semaphore_wait(barrier, 19)
    pending = []

    def go(src, dst, send, recv, dev):
        c = copy(src, dst, send, recv, dev)
        c.start()
        pending.append(c)
        return c

    k_halo = [go(kn.at[row1, rows], kprev, s_halo.at[0], r_halo.at[0], upper_dev),
              go(kn.at[row0, rows], knext, s_halo.at[1], r_halo.at[1], lower_dev)]
    top, bottom = pl.ds(PAD + PLANES - 8, 8), pl.ds(PAD, 8)
    edge = [go(kn.at[:, top], edge_in.at[0], s_edge.at[0], r_edge.at[0], n_dev(1)),
            go(kn.at[:, bottom], edge_in.at[1], s_edge.at[1], r_edge.at[1], n_dev(3)),
            go(un.at[:, top], edge_in.at[2], s_edge.at[2], r_edge.at[2], n_dev(1)),
            go(un.at[:, bottom], edge_in.at[3], s_edge.at[3], r_edge.at[3], n_dev(3))]
    u_halo = [go(un.at[row1, rows], uprev, s_halo.at[2], r_halo.at[2], upper_dev),
              go(un.at[row0, rows], unext, s_halo.at[3], r_halo.at[3], lower_dev)]

    sub8 = lax.broadcasted_iota(jnp.int32, (8, 1), 0)
    first = sub8 == 0

    def to_x(src):
        for j in range(2):
            for xt in range(2):
                work[j, pl.ds(xt * 128, 128)] = src[j * 2 + xt, rows].T

    to_x(kn)

    def xrow(ref, t):
        return jnp.concatenate(
            [ref[c, pl.ds(t, 8, stride=TX), :] for c in range(2)], axis=1)

    k_before = pltpu.roll(xrow(work, TX - 1), 1, 0)
    p = h = sigma = None
    for t in range(TX):
        k_now = xrow(work, t)
        a = face(k_before, k_now)
        k_before = k_now
        if t == 0:
            a = jnp.where(first, 0.0, a)
            p, h = jnp.ones_like(a), a
        else:
            inv = 1.0 / (p + h + a)
            hm = h * inv
            sigma = hm * p if sigma is None else sigma + hm * p
            r = a * inv
            xr[t] = r
            xi[t - 1] = inv
            xh[t - 1] = hm
            p = 1.0 + r * p
            h = r * h
    x_levels, x_inv = spread_factor(p + jnp.where(sub8 == 7, 0.0, pltpu.roll(sigma, 7, 0)), h)
    for i, (alpha, gamma) in enumerate(x_levels):
        xlev[2 * i] = alpha
        xlev[2 * i + 1] = gamma
    xlev[6] = x_inv

    for c in edge:
        c.wait_recv()
    kn[:, pl.ds(0, PAD)] = edge_in[0]
    kn[:, pl.ds(PAD + PLANES, PAD)] = edge_in[1]
    un[:, pl.ds(0, PAD)] = edge_in[2]
    un[:, pl.ds(PAD + PLANES, PAD)] = edge_in[3]
    for q in range(9):
        size = 8 if q == 8 else 16
        low = kn[:, pl.ds(PAD - 1 + q * 16, size)]
        high = kn[:, pl.ds(PAD + q * 16, size)]
        value = face(low, high)
        if q in (0, 8):
            at = lax.broadcasted_iota(jnp.int32, (size, 1), 0)
            value = jnp.where((at == 0) & (n == (0 if q == 0 else 3)), 0.0, value)
        az[:, pl.ds(PAD + q * 16, size)] = value

    p = h = sigma = None
    def zrow(ref, t):
        return jnp.concatenate([ref[c, pl.ds(t, 8, stride=TZ), :] for c in range(4)], axis=1)

    for t in range(TZ):
        a = zrow(az, PAD + t)
        if t == 0:
            p, h = jnp.ones_like(a), a
        else:
            inv = 1.0 / (p + h + a)
            hm = h * inv
            sigma = hm * p if sigma is None else sigma + hm * p
            r = a * inv
            zr[t] = r
            zi[t - 1] = inv
            zh[t - 1] = hm
            p = 1.0 + r * p
            h = r * h
    last = sub8 == 7
    mass = p + jnp.where(last, 0.0, pltpu.roll(sigma, 7, 0))
    h_up = pltpu.roll(h, 7, 0)
    low = jnp.where(first | last, 0.0, h)
    ground = mass + jnp.where(first, h, 0.0) + jnp.where(sub8 == 6, h_up, 0.0)
    levels, inverse = spread_factor(jnp.where(last, 1.0, ground), low)
    for i, (alpha, gamma) in enumerate(levels):
        zlev[2 * i] = alpha
        zlev[2 * i + 1] = gamma
    zlev[6] = inverse
    from_low = spread_solve(levels, inverse, jnp.where(first, h, 0.0))
    from_high = spread_solve(levels, inverse, jnp.where(sub8 == 6, h_up, 0.0))
    own_mass = spread_solve(levels, inverse, jnp.where(last, 0.0, mass))
    zlev[7] = from_low
    zlev[8] = from_high
    zlev[9] = h

    def pick(value, s):
        return jnp.broadcast_to(value[s:s + 1], value.shape)

    h0, h7 = pick(h, 0), pick(h, 7)
    nm_out[0] = pick(mass, 7) + h7 * pick(own_mass, 6)
    nm_out[1] = pick(sigma, 0) + h0 * pick(own_mass, 0)
    nm_out[2] = h0 * pick(from_high, 0)
    nm = [go(nm_out, nm_in.at[pl.ds(3 * (i - 1), 3)], s_n.at[0, i], r_n.at[0, i], n_dev(i))
          for i in (2, 1, 3)]

    for q in range(8):
        part, src = pl.ds(q * 16, 16), pl.ds(PAD + q * 16, 16)
        ay[1, :, part] = face(kn[row0, src], kn[row1, src])
    k_halo[0].wait_recv()
    for q in range(8):
        part, src = pl.ds(q * 16, 16), pl.ds(PAD + q * 16, 16)
        ay[0, :, part] = jnp.where(w > 0, face(kprev[:, part], kn[row0, src]), 0.0)
    mine = pl.multiple_of(core * 64, 64)
    other = pl.multiple_of(64 - core * 64, 64)
    a_core = go(ay.at[pl.ds(0, 2), :, pl.ds(other, 64)], a_other, s_core.at[0], r_core.at[0], partner)
    k_halo[1].wait_recv()
    for q in range(8):
        part, src = pl.ds(q * 16, 16), pl.ds(PAD + q * 16, 16)
        ay[2, :, part] = jnp.where(w < WIDE - 1, face(kn[row1, src], knext[:, part]), 0.0)

    a_core.wait_recv()
    swap = core == 1
    a_mine[...] = ay[pl.ds(0, 2), :, pl.ds(mine, 64)]
    for o in range(8):
        part = pl.ds(o * 8, 8)
        own, far = [a_mine[j, :, part] for j in range(2)], [a_other[j, :, part] for j in range(2)]
        sub = ([jnp.where(swap, far[j], own[j]) for j in range(2)]
               + [jnp.where(swap, own[j], far[j]) for j in range(2)])
        one = jnp.ones_like(sub[0])
        p, h, sigma, ratios, inverses, reach = forward_matrix([one] * 4, sub, None)
        zm_out[o, 0], zm_out[o, 1], zm_out[o, 2] = p, sigma, h
        for t in range(3):
            ym_r[o, t], ym_i[o, t], ym_h[o, t] = ratios[t], inverses[t], reach[t]
    zm_in[zc] = zm_out[zc]
    zm = [go(zm_out.at[lax.rem(zc + i, RING)], zm_in.at[zc], s_ring.at[0, i], r_ring.at[0, i],
             ring_dev(i)) for i in FAR]

    for c in u_halo:
        c.wait_recv()
    for q in range(8):
        part, src = pl.ds(q * 16, 16), pl.ds(PAD + q * 16, 16)
        u0, u1 = un[row0, src], un[row1, src]
        mid = ay[1, :, part] * (u1 - u0)
        ly = (mid - ay[0, :, part] * (u0 - uprev[:, part]),
              ay[2, :, part] * (unext[:, part] - u1) - mid)
        for j, (row, u) in enumerate(((row0, u0), (row1, u1))):
            up, down = pl.ds(PAD + q * 16 + 1, 16), pl.ds(PAD + q * 16 - 1, 16)
            lz = az[row, up] * (un[row, up] - u) - az[row, src] * (u - un[row, down])
            zg[row, part] = u + ly[j] + lz
    for j in range(2):
        for xt in range(2):
            work[j, pl.ds(xt * 128, 128)] = zg[j * 2 + xt].T
    g = acc = None
    for t in range(TX):
        f = xrow(work, t)
        g = f if t == 0 else f + xr[t] * g
        if t < TX - 1:
            acc = xh[t] * g if acc is None else acc + xh[t] * g
            xg[t] = g * xi[t]
    g = g + jnp.where(sub8 == 7, 0.0, pltpu.roll(acc, 7, 0))
    sep = spread_solve([(xlev[2 * i], xlev[2 * i + 1]) for i in range(3)], xlev[6], g)
    left = jnp.where(first, 0.0, pltpu.roll(sep, 1, 0))
    value = sep
    for t in range(TX - 1, -1, -1):
        if t < TX - 1:
            value = xg[t] + xh[t] * left + xr[t + 1] * value
        for c in range(2):
            work[c, pl.ds(t, 8, stride=TX), :] = value[:, c * 128:(c + 1) * 128]
    for j in range(2):
        for xt in range(2):
            back = work[j, pl.ds(xt * 128, 128)].T
            xa[j, xt] = 2.0 * (back - un[j * 2 + xt, rows])
    d_core = go(xa.at[:, :, pl.ds(other, 64)], d_other, s_core.at[1], r_core.at[1], partner)

    d_core.wait_recv()
    d_mine[...] = xa[:, :, pl.ds(mine, 64)]
    for o in range(8):
        part = pl.ds(o * 8, 8)
        own, far = [d_mine[j, :, part] for j in range(2)], [d_other[j, :, part] for j in range(2)]
        f = ([jnp.where(swap, far[j], own[j]) for j in range(2)]
             + [jnp.where(swap, own[j], far[j]) for j in range(2)])
        g, acc = f[0], None
        for t in range(3):
            y_g[o, t] = g * ym_i[o, t]
            add = ym_h[o, t] * g
            acc = add if acc is None else acc + add
            g = f[t + 1] + ym_r[o, t] * g
        zr_out[o, 0], zr_out[o, 1] = g, acc
    zr_in[zc] = zr_out[zc]
    zrc = [go(zr_out.at[lax.rem(zc + i, RING)], zr_in.at[zc], s_ring.at[1, i], r_ring.at[1, i],
              ring_dev(i)) for i in FAR]

    for c in zm:
        c.wait_recv()
    masses = [zm_in[s, 0] + zm_in[s + 1, 1] for s in range(7)] + [zm_in[7, 0]]
    p, h, sigma, ratios, inverses, reach = forward_matrix(
        masses, [zm_in[s, 2] for s in range(8)], None)
    yk_out[0], yk_out[1], yk_out[2] = p, zm_in[0, 1] + sigma, h
    for t in range(7):
        l_r[t], l_i[t], l_h[t] = ratios[t], inverses[t], reach[t]
    yk_in[yc] = yk_out[...]
    yk = [go(yk_out, yk_in.at[yc], s_col.at[0, i], r_col.at[0, i], col_dev(i)) for i in FAR]

    for c in zrc:
        c.wait_recv()
    g, acc = zr_in[0, 0] + zr_in[1, 1], None
    for s in range(7):
        l_g[s] = g * l_i[s]
        add = l_h[s] * g
        acc = add if acc is None else acc + add
        g = zr_in[s + 1, 0] + l_r[s] * g
        if s < 6:
            g = g + zr_in[s + 2, 1]
    yr_out[0], yr_out[1] = g, zr_in[0, 1] + acc
    yr_in[yc] = yr_out[...]
    yr = [go(yr_out, yr_in.at[yc], s_col.at[1, i], r_col.at[1, i], col_dev(i)) for i in FAR]

    for c in yk:
        c.wait_recv()
    masses = [yk_in[s, 0] + yk_in[s + 1, 1] for s in range(7)] + [yk_in[7, 0]]
    sub = [yk_in[s, 2] for s in range(8)]
    p, ratios, inverses = masses[0], [], []
    for s in range(1, 8):
        inv = 1.0 / (p + sub[s])
        ratios.append(sub[s] * inv)
        inverses.append(inv)
        p = masses[s] + ratios[-1] * p
    inverses.append(1.0 / p)
    for c in yr:
        c.wait_recv()
    values = [yr_in[0, 0] + yr_in[1, 1]]
    for s in range(1, 8):
        g = yr_in[s, 0] + ratios[s - 1] * values[-1]
        values.append(g + yr_in[s + 1, 1] if s < 7 else g)
    value = values[7] * inverses[7]
    sol8[8] = value
    for s in range(6, -1, -1):
        value = values[s] * inverses[s] + ratios[s] * value
        sol8[s + 1] = value
    sol8[0] = jnp.zeros_like(value)
    left, value = sol8[yc], sol8[yc + 1]
    back_out[7, 1] = value
    for s in range(6, -1, -1):
        value = l_g[s] + l_h[s] * left + l_r[s] * value
        back_out[s, 1] = value
        back_out[s + 1, 0] = value
    back_out[0, 0] = left
    back_in[zc] = back_out[zc]
    bk = [go(back_out.at[lax.rem(zc + i, RING)], back_in.at[zc], s_ring.at[2, i], r_ring.at[2, i],
             ring_dev(i)) for i in FAR]
    for c in bk:
        c.wait_recv()
    for o in range(8):
        part = pl.ds(o * 8, 8)
        left, value = back_in[o, 0], back_in[o, 1]
        solved = [None, None, None, value]
        for t in range(2, -1, -1):
            value = y_g[o, t] + ym_h[o, t] * left + ym_r[o, t] * value
            solved[t] = value
        for j in range(2):
            back_core[j, :, part] = jnp.where(swap, solved[j], solved[2 + j])
            d_mine[j, :, part] = jnp.where(swap, solved[2 + j], solved[j])
    home = go(back_core, home_core, s_core.at[2], r_core.at[2], partner)
    for j in range(2):
        zg[pl.ds(2 * j, 2), pl.ds(mine, 64)] = d_mine[j]
    home.wait_recv()
    for j in range(2):
        zg[pl.ds(2 * j, 2), pl.ds(other, 64)] = home_core[j]

    g = acc = None
    for t in range(TZ):
        f = zrow(zg, t)
        g = f if t == 0 else f + zr[t] * g
        if t < TZ - 1:
            acc = zh[t] * g if acc is None else acc + zh[t] * g
            zi[t] = g * zi[t]
    g = g + jnp.where(last, 0.0, pltpu.roll(acc, 7, 0))
    levels = [(zlev[2 * i], zlev[2 * i + 1]) for i in range(3)]
    base = spread_solve(levels, zlev[6], jnp.where(last, 0.0, g))
    h = zlev[9]
    nr_out[0] = pick(g, 7) + pick(h, 7) * pick(base, 6)
    nr_out[1] = pick(acc, 0) + pick(h, 0) * pick(base, 0)
    nr = [go(nr_out, nr_in.at[pl.ds(2 * (i - 1), 2)], s_n.at[1, i], r_n.at[1, i], n_dev(i))
          for i in (2, 1, 3)]
    for c in nm:
        c.wait_recv()

    def stacked(own, ref, offset, step):
        whole = jnp.where(sub8 == n, own, 0.0)
        for i in range(1, 4):
            whole = jnp.where(sub8 == lax.rem(n + 4 - i, 4), ref[offset + step * (i - 1)], whole)
        return whole

    top_mass, low_mass, coupling = [stacked(nm_out[v], nm_in, v, 3) for v in range(3)]
    high = pltpu.roll(coupling, 7, 0)
    mass = top_mass + jnp.where(sub8 < 3, pltpu.roll(low_mass, 7, 0), 0.0)
    mass = jnp.where(sub8 < 4, mass, 1.0)
    n_levels, n_inverse = spread_factor(mass, coupling)
    for c in nr:
        c.wait_recv()
    top_rhs, low_rhs = [stacked(nr_out[v], nr_in, v, 2) for v in range(2)]
    rhs = top_rhs + jnp.where(sub8 < 3, pltpu.roll(low_rhs, 7, 0), 0.0)
    ends = spread_solve(n_levels, n_inverse, rhs)
    mine_end = jnp.sum(jnp.where(sub8 == n, ends, 0.0), axis=0, keepdims=True)
    left_end = jnp.sum(jnp.where(sub8 == n - 1, ends, 0.0), axis=0, keepdims=True)
    sep = jnp.where(last, mine_end, base + zlev[7] * left_end + zlev[8] * mine_end)
    left = jnp.where(first, left_end, pltpu.roll(sep, 1, 0))
    value = sep
    for t in range(TZ - 1, -1, -1):
        if t < TZ - 1:
            value = zi[t] + zh[t] * left + zr[t + 1] * value
        for c in range(4):
            zg[c, pl.ds(t, 8, stride=TZ), :] = value[:, c * 128:(c + 1) * 128]
    for j in range(2):
        for xt in range(2):
            c = j * 2 + xt
            out[pl.ds(xt * 2 + j, PLANES, stride=4), :] = un[c, rows] + zg[c]
    for c in pending:
        c.wait_send()


def flat(value):
    return value.reshape(PLANES, 2, 2, 128).transpose(0, 2, 1, 3).reshape(4 * PLANES, 128)


def per_device(initial_heat_level, heat_transmission):
    f32 = jnp.float32
    V = lambda *shape: pltpu.VMEM(shape, f32)
    S = lambda *shape: pltpu.SemaphoreType.DMA(shape)
    natural = (4, PLANES + 2 * PAD, 128)
    halo = (2, PLANES, 128)
    half = (2, 2, 64, 128)
    tile = (2, 8, 128)
    scratch = [
        V(4 * PLANES, 128), V(4 * PLANES, 128), S(2),
        V(*natural), V(*natural), V(*natural),
        V(*halo), V(*halo), V(*halo), V(*halo), V(3, *halo),
        V(2, X, 128), V(TX, 8, 256), V(TX, 8, 256), V(TX, 8, 256), V(TX, 8, 256), V(2, *halo),
        V(TZ, 8, 512), V(TZ, 8, 512), V(TZ, 8, 512), V(4, PLANES, 128),
        V(*half), V(*half), V(*half), V(*half),
        V(8, 3, *tile), V(8, 3, *tile), V(8, 3, *tile), V(8, 3, *tile),
        V(8, 3, *tile), V(8, 3, *tile), V(8, 2, *tile), V(8, 2, *tile),
        V(7, *tile), V(7, *tile), V(7, *tile), V(7, *tile),
        V(3, *tile), V(8, 3, *tile), V(2, *tile), V(8, 2, *tile), V(9, *tile),
        V(8, 2, *tile), V(8, 2, *tile), V(*half), V(*half),
        V(3, 8, 512), V(9, 8, 512), V(2, 8, 512), V(6, 8, 512), V(4, 4, 8, 128),
        V(7, 8, 256), V(10, 8, 512),
        S(4), S(4), S(4), S(4), S(3), S(3), S(3, 8), S(3, 8), S(2, 8), S(2, 8), S(2, 4), S(2, 4),
    ]
    vmem = pl.BlockSpec(memory_space=pltpu.VMEM)
    hbm = pl.BlockSpec(memory_space=pltpu.HBM)
    result = pl.pallas_call(
        kernel,
        out_shape=jax.ShapeDtypeStruct((4 * PLANES, 128), f32),
        in_specs=[hbm, hbm],
        out_specs=vmem,
        scratch_shapes=scratch,
        compiler_params=pltpu.CompilerParams(
            collective_id=0, has_side_effects=True, vmem_limit_bytes=40 << 20),
    )(*[pltpu.with_memory_space_constraint(flat(v), pltpu.HBM)
        for v in (initial_heat_level, heat_transmission)])
    return result.reshape(PLANES, 2, 2, 128).transpose(0, 2, 1, 3).reshape(PLANES, 2, X)


def solution(mesh):
    spec = P("narrow", "wide", None)
    return jax.shard_map(
        per_device, mesh=mesh, in_specs=(spec, spec), out_specs=spec, check_vma=False)
```

```python
import functools

import jax
import jax.numpy as jnp
from jax import lax
from jax.experimental import pallas as pl
from jax.experimental.pallas import tpu as pltpu
from jax.sharding import PartitionSpec as P

MESH = pl.DeviceIdType.MESH
WIDE, RING, PLANES, X = 128, 8, 128, 256
PAD = 8
TX, TZ = 32, 16
FACE = 500.0
FAR = (4, 3, 5, 2, 6, 1, 7)


def face(lower, upper):
    return FACE * lower * upper / (lower + upper)


def forward_matrix(masses, sub):
    p, h = masses[0], sub[0]
    ratios, inverses, reach, sigma = [], [], [], None
    for t in range(1, len(sub)):
        inv = 1.0 / (p + h + sub[t])
        hm = h * inv
        sigma = hm * p if sigma is None else sigma + hm * p
        r = sub[t] * inv
        ratios.append(r)
        inverses.append(inv)
        reach.append(hm)
        p = masses[t] + r * p
        h = r * h
    return p, h, sigma, ratios, inverses, reach


def neighbours(value, step):
    size = value.shape[0]
    return pltpu.roll(value, step, 0), pltpu.roll(value, size - step, 0)


def spread_factor(mass, low):
    high = pltpu.roll(low, 7, 0)
    levels = []
    for step in (1, 2, 4):
        inv = 1.0 / (mass + low + high)
        inv_down, inv_up = neighbours(inv, step)
        alpha, gamma = low * inv_down, high * inv_up
        mass_down, mass_up = neighbours(mass, step)
        mass = mass + alpha * mass_down + gamma * mass_up
        low = alpha * pltpu.roll(low, step, 0)
        high = gamma * pltpu.roll(high, 8 - step, 0)
        levels.append((alpha, gamma))
    return levels, 1.0 / mass


def spread_solve(levels, inverse, value):
    for (alpha, gamma), step in zip(levels, (1, 2, 4)):
        down, up = neighbours(value, step)
        value = value + alpha * down + gamma * up
    return value * inverse


def kernel(u_hbm, k_hbm, out, u_in, k_in, s_load, un, kn, az, uprev, unext, khalo, kx, a0x, k_mine, k_inner, a_mine, d_back, ay,
           work, xr, xi, xh, xg, zr, zi, zh, zg,
           d_send, d_mine, d_other, ym_r, ym_i, ym_h, ym_0, y_g,
           zm_out, zm_in, za_out, za_in, zr_out, zr_in, l_r, l_i, l_h, l_g,
           yk_out, yk_in, yr_out, yr_in, sol8, back_out, back_in, back_core, home_core, zd,
           nm_out, nm_in, nr_out, nr_in, edge_in, xlev, zlev,
           s_halo, r_halo, s_edge, r_edge, s_core, r_core, s_ring, r_ring, s_col, r_col, s_n, r_n):
    w = lax.axis_index("wide")
    n = lax.axis_index("narrow")
    core = lax.rem(w, 2)
    zc = lax.rem(w // 2, RING)
    yc = w // (2 * RING)
    partner = {"wide": w + 1 - 2 * core}
    upper_dev = {"wide": lax.rem(w + 1, WIDE)}
    lower_dev = {"wide": lax.rem(w + WIDE - 1, WIDE)}

    def ring_dev(i):
        return {"wide": yc * (2 * RING) + lax.rem(zc + i, RING) * 2 + core}

    def col_dev(i):
        return {"wide": lax.rem(yc + i, RING) * (2 * RING) + zc * 2 + core}

    def n_dev(i):
        return {"narrow": lax.rem(n + i, 4)}

    def copy(src, dst, send, recv, dev):
        return pltpu.make_async_remote_copy(
            src_ref=src, dst_ref=dst, send_sem=send, recv_sem=recv,
            device_id=dev, device_id_type=MESH)

    loads = [pltpu.make_async_copy(k_hbm, k_in, s_load.at[0]),
             pltpu.make_async_copy(u_hbm, u_in, s_load.at[1])]
    for c in loads:
        c.start()
    barrier = pltpu.get_barrier_semaphore()
    for dev in ([upper_dev, lower_dev] + [ring_dev(i) for i in range(1, 8)]
                + [col_dev(i) for i in range(1, 8)] + [n_dev(i) for i in range(1, 4)]):
        pl.semaphore_signal(barrier, 1, device_id=dev, device_id_type=MESH)

    rows = pl.ds(PAD, PLANES)
    for c, src, dst in zip(loads, (k_in, u_in), (kn, un)):
        c.wait()
        for j in range(2):
            for xt in range(2):
                dst[j * 2 + xt, rows] = src[pl.ds(xt * 2 + j, PLANES, stride=4), :]
    row0, row1 = pl.ds(0, 2), pl.ds(2, 2)

    pl.semaphore_wait(barrier, 19)
    pending = []

    def go(src, dst, send, recv, dev):
        c = copy(src, dst, send, recv, dev)
        c.start()
        pending.append(c)
        return c

    mine = pl.multiple_of(core * 64, 64)
    other = pl.multiple_of(64 - core * 64, 64)
    halves = (other, mine)
    outer = go(kn.at[pl.ds(2 * core, 2), pl.ds(pl.multiple_of(PAD + other, 8), 64)], kx,
               s_core.at[0], r_core.at[0], partner)
    k_halo = [go(kn.at[row1, rows], khalo.at[0], s_halo.at[0], r_halo.at[0], upper_dev),
              go(kn.at[row0, rows], khalo.at[1], s_halo.at[1], r_halo.at[1], lower_dev)]
    top, bottom = pl.ds(PAD + PLANES - 8, 8), pl.ds(PAD, 8)
    edge = [go(kn.at[:, top], edge_in.at[0], s_edge.at[0], r_edge.at[0], n_dev(1)),
            go(kn.at[:, bottom], edge_in.at[1], s_edge.at[1], r_edge.at[1], n_dev(3)),
            go(un.at[:, top], edge_in.at[2], s_edge.at[2], r_edge.at[2], n_dev(1)),
            go(un.at[:, bottom], edge_in.at[3], s_edge.at[3], r_edge.at[3], n_dev(3))]
    u_halo = []
    for i, half in enumerate((mine, other)):
        src = pl.ds(pl.multiple_of(PAD + half, 8), 64)
        u_halo.append([
            go(un.at[row1, src], uprev.at[:, pl.ds(half, 64)], s_halo.at[2 + 2 * i],
               r_halo.at[2 + 2 * i], upper_dev),
            go(un.at[row0, src], unext.at[:, pl.ds(half, 64)], s_halo.at[3 + 2 * i],
               r_halo.at[3 + 2 * i], lower_dev)])

    sub8 = lax.broadcasted_iota(jnp.int32, (8, 1), 0)
    first = sub8 == 0

    def to_x(half, block):
        for xt in range(2):
            work[half, pl.ds(xt * 128, 128)] = jnp.concatenate(
                [block(j, xt) for j in range(2)], axis=0).T

    for half in range(2):
        part = pl.ds(pl.multiple_of(PAD + halves[half], 8), 64)
        to_x(half, lambda j, xt: kn[j * 2 + xt, part])

    def xrow(ref, t):
        return jnp.concatenate(
            [ref[c, pl.ds(t, 8, stride=TX), :] for c in range(2)], axis=1)

    k_before = pltpu.roll(xrow(work, TX - 1), 1, 0)
    p = h = sigma = None
    for t in range(TX):
        k_now = xrow(work, t)
        a = face(k_before, k_now)
        k_before = k_now
        if t == 0:
            a = jnp.where(first, 0.0, a)
            p, h = jnp.ones_like(a), a
        else:
            inv = 1.0 / (p + h + a)
            hm = h * inv
            sigma = hm * p if sigma is None else sigma + hm * p
            r = a * inv
            xr[t] = r
            xi[t - 1] = inv
            xh[t - 1] = hm
            p = 1.0 + r * p
            h = r * h
    x_levels, x_inv = spread_factor(p + jnp.where(sub8 == 7, 0.0, pltpu.roll(sigma, 7, 0)), h)
    for i, (alpha, gamma) in enumerate(x_levels):
        xlev[2 * i] = alpha
        xlev[2 * i + 1] = gamma
    xlev[6] = x_inv

    for c in edge:
        c.wait_recv()
    kn[:, pl.ds(0, PAD)] = edge_in[0]
    kn[:, pl.ds(PAD + PLANES, PAD)] = edge_in[1]
    un[:, pl.ds(0, PAD)] = edge_in[2]
    un[:, pl.ds(PAD + PLANES, PAD)] = edge_in[3]
    for q in range(9):
        size = 8 if q == 8 else 16
        low = kn[:, pl.ds(PAD - 1 + q * 16, size)]
        high = kn[:, pl.ds(PAD + q * 16, size)]
        value = face(low, high)
        if q in (0, 8):
            at = lax.broadcasted_iota(jnp.int32, (size, 1), 0)
            value = jnp.where((at == 0) & (n == (0 if q == 0 else 3)), 0.0, value)
        az[:, pl.ds(PAD + q * 16, size)] = value

    swap = core == 1
    outer.wait_recv()
    pltpu.make_async_copy(khalo.at[0], khalo.at[0], r_halo.at[1 - core]).wait()
    k_mine[...] = kn[:, pl.ds(pl.multiple_of(PAD + mine, 8), 64)]
    k_inner[...] = khalo[1 - core, :, pl.ds(mine, 64)]
    for o in range(8):
        here = pl.ds(o * 8, 8)
        own = [k_mine[pl.ds(2 * j, 2), here] for j in range(2)]
        inner = k_inner[:, here]
        outside = kx[:, here]
        cells = [jnp.where(swap, outside, own[0]), jnp.where(swap, inner, own[1]),
                 jnp.where(swap, own[0], inner), jnp.where(swap, own[1], outside)]
        one = jnp.ones_like(inner)
        p, h, sigma, ratios, inverses, reach = forward_matrix(
            [one] * 3, [face(cells[t], cells[t + 1]) for t in range(3)])
        zm_out[o, 0], zm_out[o, 1], zm_out[o, 2] = 1.0 + sigma, h, p
        for t in range(2):
            ym_r[o, t], ym_i[o, t], ym_h[o, t] = ratios[t], inverses[t], reach[t]
    zm_in[zc] = zm_out[zc]
    zm = [go(zm_out.at[lax.rem(zc + i, RING)], zm_in.at[zc], s_ring.at[0, i], r_ring.at[0, i],
             ring_dev(i)) for i in FAR]

    for q in range(8):
        part, src = pl.ds(q * 16, 16), pl.ds(PAD + q * 16, 16)
        mid = face(kn[row0, src], kn[row1, src])
        ay[1, :, part] = mid
        flux = mid * (un[row1, src] - un[row0, src])
        for row, flow in ((row0, flux), (row1, -flux)):
            u = un[row, src]
            up, down = pl.ds(PAD + q * 16 + 1, 16), pl.ds(PAD + q * 16 - 1, 16)
            lz = az[row, up] * (un[row, up] - u) - az[row, src] * (u - un[row, down])
            zg[row, part] = u + lz + flow

    p = h = sigma = None
    def zrow(ref, t):
        return jnp.concatenate([ref[c, pl.ds(t, 8, stride=TZ), :] for c in range(4)], axis=1)

    for t in range(TZ):
        a = zrow(az, PAD + t)
        if t == 0:
            p, h = jnp.ones_like(a), a
        else:
            inv = 1.0 / (p + h + a)
            hm = h * inv
            sigma = hm * p if sigma is None else sigma + hm * p
            r = a * inv
            zr[t] = r
            zi[t - 1] = inv
            zh[t - 1] = hm
            p = 1.0 + r * p
            h = r * h
    last = sub8 == 7
    mass = p + jnp.where(last, 0.0, pltpu.roll(sigma, 7, 0))
    h_up = pltpu.roll(h, 7, 0)
    low = jnp.where(first | last, 0.0, h)
    ground = mass + jnp.where(first, h, 0.0) + jnp.where(sub8 == 6, h_up, 0.0)
    levels, inverse = spread_factor(jnp.where(last, 1.0, ground), low)
    for i, (alpha, gamma) in enumerate(levels):
        zlev[2 * i] = alpha
        zlev[2 * i + 1] = gamma
    zlev[6] = inverse
    from_low = spread_solve(levels, inverse, jnp.where(first, h, 0.0))
    from_high = spread_solve(levels, inverse, jnp.where(sub8 == 6, h_up, 0.0))
    own_mass = spread_solve(levels, inverse, jnp.where(last, 0.0, mass))
    zlev[7] = from_low
    zlev[8] = from_high
    zlev[9] = h

    def pick(value, s):
        return jnp.broadcast_to(value[s:s + 1], value.shape)

    h0, h7 = pick(h, 0), pick(h, 7)
    nm_out[0] = pick(mass, 7) + h7 * pick(own_mass, 6)
    nm_out[1] = pick(sigma, 0) + h0 * pick(own_mass, 0)
    nm_out[2] = h0 * pick(from_high, 0)
    nm = [go(nm_out, nm_in.at[pl.ds(3 * (i - 1), 3)], s_n.at[0, i], r_n.at[0, i], n_dev(i))
          for i in (2, 1, 3)]

    pltpu.make_async_copy(khalo.at[0], khalo.at[0], r_halo.at[core]).wait()
    for q in range(8):
        part, src = pl.ds(q * 16, 16), pl.ds(PAD + q * 16, 16)
        ay[0, :, part] = jnp.where(w > 0, face(khalo[0, :, part], kn[row0, src]), 0.0)
    a_core = go(ay.at[0, :, pl.ds(other, 64)], a0x, s_core.at[3], r_core.at[3], partner)
    for q in range(8):
        part, src = pl.ds(q * 16, 16), pl.ds(PAD + q * 16, 16)
        ay[2, :, part] = jnp.where(w < WIDE - 1, face(kn[row1, src], khalo[1, :, part]), 0.0)

    def solve_x(half, target):
        at = halves[half]
        src = pl.ds(pl.multiple_of(PAD + at, 8), 64)
        part = pl.ds(at, 64)
        for c in u_halo[half]:
            c.wait_recv()

        def rhs(j, xt):
            if j == 0:
                return zg[xt, part] - ay[0, xt, part] * (un[xt, src] - uprev[xt, part])
            return zg[2 + xt, part] + ay[2, xt, part] * (unext[xt, part] - un[2 + xt, src])

        to_x(half, rhs)
        lane = pl.ds(half * 128, 128)
        g = acc = None
        for t in range(TX):
            f = work[half, pl.ds(t, 8, stride=TX), :]
            g = f if t == 0 else f + xr[t, :, lane] * g
            if t < TX - 1:
                acc = xh[t, :, lane] * g if acc is None else acc + xh[t, :, lane] * g
                xg[t] = g * xi[t, :, lane]
        g = g + jnp.where(sub8 == 7, 0.0, pltpu.roll(acc, 7, 0))
        sep = spread_solve([(xlev[2 * i, :, lane], xlev[2 * i + 1, :, lane]) for i in range(3)],
                           xlev[6, :, lane], g)
        left = jnp.where(first, 0.0, pltpu.roll(sep, 1, 0))
        value = sep
        for t in range(TX - 1, -1, -1):
            if t < TX - 1:
                value = xg[t] + xh[t, :, lane] * left + xr[t + 1, :, lane] * value
            work[half, pl.ds(t, 8, stride=TX), :] = value
        for xt in range(2):
            back = work[half, pl.ds(xt * 128, 128)].T
            for j in range(2):
                target[j, xt] = 2.0 * (back[j * 64:(j + 1) * 64] - un[j * 2 + xt, src])

    a_core.wait_recv()
    a_mine[...] = ay[0, :, pl.ds(mine, 64)]
    for o in range(8):
        here = pl.ds(o * 8, 8)
        za_out[o] = jnp.where(swap, a0x[:, here], a_mine[:, here])
    za_in[zc] = za_out[zc]
    za = [go(za_out.at[lax.rem(zc + i, RING)], za_in.at[zc], s_ring.at[3, i], r_ring.at[3, i],
             ring_dev(i)) for i in FAR]

    solve_x(0, d_send)
    d_core = go(d_send, d_other, s_core.at[1], r_core.at[1], partner)

    for o in range(8):
        a, h = za_out[o], zm_out[o, 1]
        inv = 1.0 / (zm_out[o, 0] + a + h)
        ym_0[o, 0], ym_0[o, 1], ym_0[o, 2] = inv, a * inv, h * inv
    solve_x(1, d_mine)
    d_core.wait_recv()
    for o in range(8):
        part = pl.ds(o * 8, 8)
        own, far = [d_mine[j, :, part] for j in range(2)], [d_other[j, :, part] for j in range(2)]
        f = ([jnp.where(swap, far[j], own[j]) for j in range(2)]
             + [jnp.where(swap, own[j], far[j]) for j in range(2)])
        g, acc = f[1], f[0]
        for t in range(2):
            y_g[o, t] = g * ym_i[o, t]
            acc = acc + ym_h[o, t] * g
            g = f[t + 2] + ym_r[o, t] * g
        y_g[o, 2] = acc * ym_0[o, 0]
        zr_out[o, 0], zr_out[o, 1] = g + ym_0[o, 2] * acc, ym_0[o, 1] * acc
    zr_in[zc] = zr_out[zc]
    zrc = [go(zr_out.at[lax.rem(zc + i, RING)], zr_in.at[zc], s_ring.at[1, i], r_ring.at[1, i],
              ring_dev(i)) for i in FAR]

    for c in zm + za:
        c.wait_recv()
    chips = []
    for s in range(8):
        low, h, high, a = zm_in[s, 0], zm_in[s, 1], zm_in[s, 2], za_in[s]
        inv = 1.0 / (low + a + h)
        up, down = h * inv, a * inv
        chips.append((high + up * low, down * low, down * h))
    masses = [chips[s][0] + chips[s + 1][1] for s in range(7)] + [chips[7][0]]
    p, h, sigma, ratios, inverses, reach = forward_matrix(
        masses, [c[2] for c in chips])
    yk_out[0], yk_out[1], yk_out[2] = p, chips[0][1] + sigma, h
    for t in range(7):
        l_r[t], l_i[t], l_h[t] = ratios[t], inverses[t], reach[t]
    yk_in[yc] = yk_out[...]
    yk = [go(yk_out, yk_in.at[yc], s_col.at[0, i], r_col.at[0, i], col_dev(i)) for i in FAR]

    for c in zrc:
        c.wait_recv()
    g, acc = zr_in[0, 0] + zr_in[1, 1], None
    for s in range(7):
        l_g[s] = g * l_i[s]
        add = l_h[s] * g
        acc = add if acc is None else acc + add
        g = zr_in[s + 1, 0] + l_r[s] * g
        if s < 6:
            g = g + zr_in[s + 2, 1]
    yr_out[0], yr_out[1] = g, zr_in[0, 1] + acc
    yr_in[yc] = yr_out[...]
    yr = [go(yr_out, yr_in.at[yc], s_col.at[1, i], r_col.at[1, i], col_dev(i)) for i in FAR]

    for c in yk:
        c.wait_recv()
    masses = [yk_in[s, 0] + yk_in[s + 1, 1] for s in range(7)] + [yk_in[7, 0]]
    sub = [yk_in[s, 2] for s in range(8)]
    p, ratios, inverses = masses[0], [], []
    for s in range(1, 8):
        inv = 1.0 / (p + sub[s])
        ratios.append(sub[s] * inv)
        inverses.append(inv)
        p = masses[s] + ratios[-1] * p
    inverses.append(1.0 / p)
    for c in yr:
        c.wait_recv()
    values = [yr_in[0, 0] + yr_in[1, 1]]
    for s in range(1, 8):
        g = yr_in[s, 0] + ratios[s - 1] * values[-1]
        values.append(g + yr_in[s + 1, 1] if s < 7 else g)
    value = values[7] * inverses[7]
    sol8[8] = value
    for s in range(6, -1, -1):
        value = values[s] * inverses[s] + ratios[s] * value
        sol8[s + 1] = value
    sol8[0] = jnp.zeros_like(value)
    left, value = sol8[yc], sol8[yc + 1]
    back_out[7, 1] = value
    for s in range(6, -1, -1):
        value = l_g[s] + l_h[s] * left + l_r[s] * value
        back_out[s, 1] = value
        back_out[s + 1, 0] = value
    back_out[0, 0] = left
    back_in[zc] = back_out[zc]
    bk = [go(back_out.at[lax.rem(zc + i, RING)], back_in.at[zc], s_ring.at[2, i], r_ring.at[2, i],
             ring_dev(i)) for i in FAR]
    for c in bk:
        c.wait_recv()
    for o in range(8):
        part = pl.ds(o * 8, 8)
        left, value = back_in[o, 0], back_in[o, 1]
        start = y_g[o, 2] + ym_0[o, 1] * left + ym_0[o, 2] * value
        third = y_g[o, 1] + ym_h[o, 1] * start + ym_r[o, 1] * value
        solved = [start, y_g[o, 0] + ym_h[o, 0] * start + ym_r[o, 0] * third, third, value]
        for j in range(2):
            back_core[pl.ds(2 * j, 2), part] = jnp.where(swap, solved[j], solved[2 + j])
            d_back[pl.ds(2 * j, 2), part] = jnp.where(swap, solved[2 + j], solved[j])
    home = go(back_core, home_core, s_core.at[2], r_core.at[2], partner)
    zd[:, pl.ds(mine, 64)] = d_back[...]
    home.wait_recv()
    zd[:, pl.ds(other, 64)] = home_core[...]

    g = acc = None
    for t in range(TZ):
        f = zrow(zd, t)
        g = f if t == 0 else f + zr[t] * g
        if t < TZ - 1:
            acc = zh[t] * g if acc is None else acc + zh[t] * g
            zi[t] = g * zi[t]
    g = g + jnp.where(last, 0.0, pltpu.roll(acc, 7, 0))
    levels = [(zlev[2 * i], zlev[2 * i + 1]) for i in range(3)]
    base = spread_solve(levels, zlev[6], jnp.where(last, 0.0, g))
    h = zlev[9]
    nr_out[0] = pick(g, 7) + pick(h, 7) * pick(base, 6)
    nr_out[1] = pick(acc, 0) + pick(h, 0) * pick(base, 0)
    nr = [go(nr_out, nr_in.at[pl.ds(2 * (i - 1), 2)], s_n.at[1, i], r_n.at[1, i], n_dev(i))
          for i in (2, 1, 3)]
    for c in nm:
        c.wait_recv()

    def stacked(own, ref, offset, step):
        whole = jnp.where(sub8 == n, own, 0.0)
        for i in range(1, 4):
            whole = jnp.where(sub8 == lax.rem(n + 4 - i, 4), ref[offset + step * (i - 1)], whole)
        return whole

    top_mass, low_mass, coupling = [stacked(nm_out[v], nm_in, v, 3) for v in range(3)]
    high = pltpu.roll(coupling, 7, 0)
    mass = top_mass + jnp.where(sub8 < 3, pltpu.roll(low_mass, 7, 0), 0.0)
    mass = jnp.where(sub8 < 4, mass, 1.0)
    n_levels, n_inverse = spread_factor(mass, coupling)
    for c in nr:
        c.wait_recv()
    top_rhs, low_rhs = [stacked(nr_out[v], nr_in, v, 2) for v in range(2)]
    rhs = top_rhs + jnp.where(sub8 < 3, pltpu.roll(low_rhs, 7, 0), 0.0)
    ends = spread_solve(n_levels, n_inverse, rhs)
    mine_end = jnp.sum(jnp.where(sub8 == n, ends, 0.0), axis=0, keepdims=True)
    left_end = jnp.sum(jnp.where(sub8 == n - 1, ends, 0.0), axis=0, keepdims=True)
    sep = jnp.where(last, mine_end, base + zlev[7] * left_end + zlev[8] * mine_end)
    left = jnp.where(first, left_end, pltpu.roll(sep, 1, 0))
    value = sep
    for t in range(TZ - 1, -1, -1):
        if t < TZ - 1:
            value = zi[t] + zh[t] * left + zr[t + 1] * value
        for c in range(4):
            zg[c, pl.ds(t, 8, stride=TZ), :] = value[:, c * 128:(c + 1) * 128]
    for j in range(2):
        for xt in range(2):
            c = j * 2 + xt
            out[pl.ds(xt * 2 + j, PLANES, stride=4), :] = un[c, rows] + zg[c]
    for c in pending:
        c.wait_send()


def flat(value):
    return value.reshape(PLANES, 2, 2, 128).transpose(0, 2, 1, 3).reshape(4 * PLANES, 128)


def per_device(initial_heat_level, heat_transmission):
    f32 = jnp.float32
    V = lambda *shape: pltpu.VMEM(shape, f32)
    S = lambda *shape: pltpu.SemaphoreType.DMA(shape)
    natural = (4, PLANES + 2 * PAD, 128)
    halo = (2, PLANES, 128)
    half = (2, 2, 64, 128)
    tile = (2, 8, 128)
    scratch = [
        V(4 * PLANES, 128), V(4 * PLANES, 128), S(2),
        V(*natural), V(*natural), V(*natural),
        V(*halo), V(*halo), V(2, *halo), V(2, 64, 128), V(2, 64, 128),
        V(4, 64, 128), V(2, 64, 128), V(2, 64, 128), V(4, 64, 128), V(3, *halo),
        V(2, X, 128), V(TX, 8, 256), V(TX, 8, 256), V(TX, 8, 256), V(TX, 8, 128),
        V(TZ, 8, 512), V(TZ, 8, 512), V(TZ, 8, 512), V(4, PLANES, 128),
        V(*half), V(*half), V(*half),
        V(8, 3, *tile), V(8, 3, *tile), V(8, 3, *tile), V(8, 3, *tile), V(8, 3, *tile),
        V(8, 3, *tile), V(8, 3, *tile), V(8, *tile), V(8, *tile), V(8, 2, *tile), V(8, 2, *tile),
        V(7, *tile), V(7, *tile), V(7, *tile), V(7, *tile),
        V(3, *tile), V(8, 3, *tile), V(2, *tile), V(8, 2, *tile), V(9, *tile),
        V(8, 2, *tile), V(8, 2, *tile), V(4, 64, 128), V(4, 64, 128), V(4, PLANES, 128),
        V(3, 8, 512), V(9, 8, 512), V(2, 8, 512), V(6, 8, 512), V(4, 4, 8, 128),
        V(7, 8, 256), V(10, 8, 512),
        S(6), S(6), S(4), S(4), S(4), S(4), S(4, 8), S(4, 8), S(2, 8), S(2, 8), S(2, 4), S(2, 4),
    ]
    vmem = pl.BlockSpec(memory_space=pltpu.VMEM)
    hbm = pl.BlockSpec(memory_space=pltpu.HBM)
    result = pl.pallas_call(
        kernel,
        out_shape=jax.ShapeDtypeStruct((4 * PLANES, 128), f32),
        in_specs=[hbm, hbm],
        out_specs=vmem,
        scratch_shapes=scratch,
        compiler_params=pltpu.CompilerParams(
            collective_id=0, has_side_effects=True, vmem_limit_bytes=40 << 20),
    )(*[pltpu.with_memory_space_constraint(flat(v), pltpu.HBM)
        for v in (initial_heat_level, heat_transmission)])
    return result.reshape(PLANES, 2, 2, 128).transpose(0, 2, 1, 3).reshape(PLANES, 2, X)


def solution(mesh):
    spec = P("narrow", "wide", None)
    return jax.shard_map(
        per_device, mesh=mesh, in_specs=(spec, spec), out_specs=spec, check_vma=False)
```

```python
import functools

import jax
import jax.numpy as jnp
from jax import lax
from jax.experimental import pallas as pl
from jax.experimental.pallas import tpu as pltpu
from jax.sharding import PartitionSpec as P

MESH = pl.DeviceIdType.MESH
WIDE, RING, PLANES, X = 128, 8, 128, 256
PAD = 8
TX, TZ = 32, 16
FACE = 500.0
FAR = (4, 3, 5, 2, 6, 1, 7)


def face(lower, upper):
    return FACE * lower * upper / (lower + upper)


def forward_matrix(masses, sub):
    p, h = masses[0], sub[0]
    ratios, inverses, reach, sigma = [], [], [], None
    for t in range(1, len(sub)):
        inv = 1.0 / (p + h + sub[t])
        hm = h * inv
        sigma = hm * p if sigma is None else sigma + hm * p
        r = sub[t] * inv
        ratios.append(r)
        inverses.append(inv)
        reach.append(hm)
        p = masses[t] + r * p
        h = r * h
    return p, h, sigma, ratios, inverses, reach


def neighbours(value, step):
    size = value.shape[0]
    return pltpu.roll(value, step, 0), pltpu.roll(value, size - step, 0)


def spread_factor(mass, low):
    high = pltpu.roll(low, 7, 0)
    levels = []
    for step in (1, 2, 4):
        inv = 1.0 / (mass + low + high)
        inv_down, inv_up = neighbours(inv, step)
        alpha, gamma = low * inv_down, high * inv_up
        mass_down, mass_up = neighbours(mass, step)
        mass = mass + alpha * mass_down + gamma * mass_up
        low = alpha * pltpu.roll(low, step, 0)
        high = gamma * pltpu.roll(high, 8 - step, 0)
        levels.append((alpha, gamma))
    return levels, 1.0 / mass


def spread_solve(levels, inverse, value):
    for (alpha, gamma), step in zip(levels, (1, 2, 4)):
        down, up = neighbours(value, step)
        value = value + alpha * down + gamma * up
    return value * inverse


def kernel(u_hbm, k_hbm, out, u_in, k_in, s_load, un, kn, az, uprev, unext, khalo, kx, a0x, k_mine, k_inner, a_mine, d_back, ay,
           work, xr, xi, xh, xg, zr, zi, zh, zg,
           d_send, d_mine, d_other, ym_r, ym_i, ym_h, ym_0, y_g,
           zm_out, zm_in, za_out, za_in, zr_out, zr_in, l_r, l_i, l_h, l_g,
           yk_out, yk_in, yr_out, yr_in, sol8, back_out, back_in, back_core, home_core, zd,
           nm_own, nm_out, nm_in, nr_own, nr_out, nr_in, edge_in, xlev, zlev,
           s_halo, r_halo, s_edge, r_edge, s_core, r_core, s_ring, r_ring, s_col, r_col, s_n, r_n):
    w = lax.axis_index("wide")
    n = lax.axis_index("narrow")
    core = lax.rem(w, 2)
    zc = lax.rem(w // 2, RING)
    yc = w // (2 * RING)
    partner = {"wide": w + 1 - 2 * core}
    upper_dev = {"wide": lax.rem(w + 1, WIDE)}
    lower_dev = {"wide": lax.rem(w + WIDE - 1, WIDE)}

    def ring_dev(i):
        return {"wide": yc * (2 * RING) + lax.rem(zc + i, RING) * 2 + core}

    def col_dev(i):
        return {"wide": lax.rem(yc + i, RING) * (2 * RING) + zc * 2 + core}

    def n_dev(i):
        return {"narrow": lax.rem(n + i, 4)}

    def copy(src, dst, send, recv, dev):
        return pltpu.make_async_remote_copy(
            src_ref=src, dst_ref=dst, send_sem=send, recv_sem=recv,
            device_id=dev, device_id_type=MESH)

    loads = [pltpu.make_async_copy(k_hbm, k_in, s_load.at[0]),
             pltpu.make_async_copy(u_hbm, u_in, s_load.at[1])]
    for c in loads:
        c.start()
    barrier = pltpu.get_barrier_semaphore()
    for dev in ([upper_dev, lower_dev] + [ring_dev(i) for i in range(1, 8)]
                + [col_dev(i) for i in range(1, 8)] + [n_dev(i) for i in range(1, 4)]):
        pl.semaphore_signal(barrier, 1, device_id=dev, device_id_type=MESH)

    rows = pl.ds(PAD, PLANES)
    for c, src, dst in zip(loads, (k_in, u_in), (kn, un)):
        c.wait()
        for j in range(2):
            for xt in range(2):
                dst[j * 2 + xt, rows] = src[pl.ds(xt * 2 + j, PLANES, stride=4), :]
    row0, row1 = pl.ds(0, 2), pl.ds(2, 2)

    pl.semaphore_wait(barrier, 19)
    pending = []

    def go(src, dst, send, recv, dev):
        c = copy(src, dst, send, recv, dev)
        c.start()
        pending.append(c)
        return c

    mine = pl.multiple_of(core * 64, 64)
    other = pl.multiple_of(64 - core * 64, 64)
    halves = (other, mine)
    outer = go(kn.at[pl.ds(2 * core, 2), pl.ds(pl.multiple_of(PAD + other, 8), 64)], kx,
               s_core.at[0], r_core.at[0], partner)
    k_halo = [go(kn.at[row1, rows], khalo.at[0], s_halo.at[0], r_halo.at[0], upper_dev),
              go(kn.at[row0, rows], khalo.at[1], s_halo.at[1], r_halo.at[1], lower_dev)]
    top, bottom = pl.ds(PAD + PLANES - 8, 8), pl.ds(PAD, 8)
    edge = [go(kn.at[:, top], edge_in.at[0], s_edge.at[0], r_edge.at[0], n_dev(1)),
            go(kn.at[:, bottom], edge_in.at[1], s_edge.at[1], r_edge.at[1], n_dev(3)),
            go(un.at[:, top], edge_in.at[2], s_edge.at[2], r_edge.at[2], n_dev(1)),
            go(un.at[:, bottom], edge_in.at[3], s_edge.at[3], r_edge.at[3], n_dev(3))]
    u_halo = []
    for i, half in enumerate((mine, other)):
        src = pl.ds(pl.multiple_of(PAD + half, 8), 64)
        u_halo.append([
            go(un.at[row1, src], uprev.at[:, pl.ds(half, 64)], s_halo.at[2 + 2 * i],
               r_halo.at[2 + 2 * i], upper_dev),
            go(un.at[row0, src], unext.at[:, pl.ds(half, 64)], s_halo.at[3 + 2 * i],
               r_halo.at[3 + 2 * i], lower_dev)])

    sub8 = lax.broadcasted_iota(jnp.int32, (8, 1), 0)
    first = sub8 == 0

    def to_x(half, block):
        for xt in range(2):
            work[half, pl.ds(xt * 128, 128)] = jnp.concatenate(
                [block(j, xt) for j in range(2)], axis=0).T

    for half in range(2):
        part = pl.ds(pl.multiple_of(PAD + halves[half], 8), 64)
        to_x(half, lambda j, xt: kn[j * 2 + xt, part])

    def xrow(ref, t):
        return jnp.concatenate(
            [ref[c, pl.ds(t, 8, stride=TX), :] for c in range(2)], axis=1)

    k_before = pltpu.roll(xrow(work, TX - 1), 1, 0)
    p = h = sigma = None
    for t in range(TX):
        k_now = xrow(work, t)
        a = face(k_before, k_now)
        k_before = k_now
        if t == 0:
            a = jnp.where(first, 0.0, a)
            p, h = jnp.ones_like(a), a
        else:
            inv = 1.0 / (p + h + a)
            hm = h * inv
            sigma = hm * p if sigma is None else sigma + hm * p
            r = a * inv
            xr[t] = r
            xi[t - 1] = inv
            xh[t - 1] = hm
            p = 1.0 + r * p
            h = r * h
    x_levels, x_inv = spread_factor(p + jnp.where(sub8 == 7, 0.0, pltpu.roll(sigma, 7, 0)), h)
    for i, (alpha, gamma) in enumerate(x_levels):
        xlev[2 * i] = alpha
        xlev[2 * i + 1] = gamma
    xlev[6] = x_inv

    for c in edge:
        c.wait_recv()
    kn[:, pl.ds(0, PAD)] = edge_in[0]
    kn[:, pl.ds(PAD + PLANES, PAD)] = edge_in[1]
    un[:, pl.ds(0, PAD)] = edge_in[2]
    un[:, pl.ds(PAD + PLANES, PAD)] = edge_in[3]
    for q in range(9):
        size = 8 if q == 8 else 16
        low = kn[:, pl.ds(PAD - 1 + q * 16, size)]
        high = kn[:, pl.ds(PAD + q * 16, size)]
        value = face(low, high)
        if q in (0, 8):
            at = lax.broadcasted_iota(jnp.int32, (size, 1), 0)
            value = jnp.where((at == 0) & (n == (0 if q == 0 else 3)), 0.0, value)
        az[:, pl.ds(PAD + q * 16, size)] = value

    swap = core == 1
    outer.wait_recv()
    pltpu.make_async_copy(khalo.at[0], khalo.at[0], r_halo.at[1 - core]).wait()
    k_mine[...] = kn[:, pl.ds(pl.multiple_of(PAD + mine, 8), 64)]
    k_inner[...] = khalo[1 - core, :, pl.ds(mine, 64)]
    for o in range(8):
        here = pl.ds(o * 8, 8)
        own = [k_mine[pl.ds(2 * j, 2), here] for j in range(2)]
        inner = k_inner[:, here]
        outside = kx[:, here]
        cells = [jnp.where(swap, outside, own[0]), jnp.where(swap, inner, own[1]),
                 jnp.where(swap, own[0], inner), jnp.where(swap, own[1], outside)]
        one = jnp.ones_like(inner)
        p, h, sigma, ratios, inverses, reach = forward_matrix(
            [one] * 3, [face(cells[t], cells[t + 1]) for t in range(3)])
        zm_out[o, 0], zm_out[o, 1], zm_out[o, 2] = 1.0 + sigma, h, p
        for t in range(2):
            ym_r[o, t], ym_i[o, t], ym_h[o, t] = ratios[t], inverses[t], reach[t]
    zm_in[zc] = zm_out[zc]
    zm = [go(zm_out.at[lax.rem(zc + i, RING)], zm_in.at[zc], s_ring.at[0, i], r_ring.at[0, i],
             ring_dev(i)) for i in FAR]

    for q in range(8):
        part, src = pl.ds(q * 16, 16), pl.ds(PAD + q * 16, 16)
        mid = face(kn[row0, src], kn[row1, src])
        ay[1, :, part] = mid
        flux = mid * (un[row1, src] - un[row0, src])
        for row, flow in ((row0, flux), (row1, -flux)):
            u = un[row, src]
            up, down = pl.ds(PAD + q * 16 + 1, 16), pl.ds(PAD + q * 16 - 1, 16)
            lz = az[row, up] * (un[row, up] - u) - az[row, src] * (u - un[row, down])
            zg[row, part] = u + lz + flow

    p = h = sigma = None
    def zrow(ref, t):
        return jnp.concatenate([ref[c, pl.ds(t, 8, stride=TZ), :] for c in range(4)], axis=1)

    for t in range(TZ):
        a = zrow(az, PAD + t)
        if t == 0:
            p, h = jnp.ones_like(a), a
        else:
            inv = 1.0 / (p + h + a)
            hm = h * inv
            sigma = hm * p if sigma is None else sigma + hm * p
            r = a * inv
            zr[t] = r
            zi[t - 1] = inv
            zh[t - 1] = hm
            p = 1.0 + r * p
            h = r * h
    last = sub8 == 7
    mass = p + jnp.where(last, 0.0, pltpu.roll(sigma, 7, 0))
    h_up = pltpu.roll(h, 7, 0)
    low = jnp.where(first | last, 0.0, h)
    ground = mass + jnp.where(first, h, 0.0) + jnp.where(sub8 == 6, h_up, 0.0)
    levels, inverse = spread_factor(jnp.where(last, 1.0, ground), low)
    for i, (alpha, gamma) in enumerate(levels):
        zlev[2 * i] = alpha
        zlev[2 * i + 1] = gamma
    zlev[6] = inverse
    from_low = spread_solve(levels, inverse, jnp.where(first, h, 0.0))
    from_high = spread_solve(levels, inverse, jnp.where(sub8 == 6, h_up, 0.0))
    own_mass = spread_solve(levels, inverse, jnp.where(last, 0.0, mass))
    zlev[7] = from_low
    zlev[8] = from_high
    zlev[9] = h

    def pick(value, s):
        return jnp.broadcast_to(value[s:s + 1], value.shape)

    h0, h7 = pick(h, 0), pick(h, 7)
    nm_own[0] = pick(mass, 7) + h7 * pick(own_mass, 6)
    nm_own[1] = pick(sigma, 0) + h0 * pick(own_mass, 0)
    nm_own[2] = h0 * pick(from_high, 0)

    def compact(own, target, count):
        for v in range(count):
            for c in range(4):
                target[pl.ds(4 * v + c, 1), :] = own[v, pl.ds(0, 1), pl.ds(c * 128, 128)]

    nm_out[pl.ds(8, 8), :] = jnp.zeros((8, 128), jnp.float32)
    compact(nm_own, nm_out, 3)
    nm = [go(nm_out, nm_in.at[i - 1], s_n.at[0, i], r_n.at[0, i], n_dev(i))
          for i in (2, 1, 3)]

    pltpu.make_async_copy(khalo.at[0], khalo.at[0], r_halo.at[core]).wait()
    for q in range(8):
        part, src = pl.ds(q * 16, 16), pl.ds(PAD + q * 16, 16)
        ay[0, :, part] = jnp.where(w > 0, face(khalo[0, :, part], kn[row0, src]), 0.0)
    a_core = go(ay.at[0, :, pl.ds(other, 64)], a0x, s_core.at[3], r_core.at[3], partner)
    for q in range(8):
        part, src = pl.ds(q * 16, 16), pl.ds(PAD + q * 16, 16)
        ay[2, :, part] = jnp.where(w < WIDE - 1, face(kn[row1, src], khalo[1, :, part]), 0.0)

    def solve_x(half, target):
        at = halves[half]
        src = pl.ds(pl.multiple_of(PAD + at, 8), 64)
        part = pl.ds(at, 64)
        for c in u_halo[half]:
            c.wait_recv()

        def rhs(j, xt):
            if j == 0:
                return zg[xt, part] - ay[0, xt, part] * (un[xt, src] - uprev[xt, part])
            return zg[2 + xt, part] + ay[2, xt, part] * (unext[xt, part] - un[2 + xt, src])

        to_x(half, rhs)
        lane = pl.ds(half * 128, 128)
        g = acc = None
        for t in range(TX):
            f = work[half, pl.ds(t, 8, stride=TX), :]
            g = f if t == 0 else f + xr[t, :, lane] * g
            if t < TX - 1:
                acc = xh[t, :, lane] * g if acc is None else acc + xh[t, :, lane] * g
                xg[t] = g * xi[t, :, lane]
        g = g + jnp.where(sub8 == 7, 0.0, pltpu.roll(acc, 7, 0))
        sep = spread_solve([(xlev[2 * i, :, lane], xlev[2 * i + 1, :, lane]) for i in range(3)],
                           xlev[6, :, lane], g)
        left = jnp.where(first, 0.0, pltpu.roll(sep, 1, 0))
        value = sep
        for t in range(TX - 1, -1, -1):
            if t < TX - 1:
                value = xg[t] + xh[t, :, lane] * left + xr[t + 1, :, lane] * value
            work[half, pl.ds(t, 8, stride=TX), :] = value
        for xt in range(2):
            back = work[half, pl.ds(xt * 128, 128)].T
            for j in range(2):
                target[j, xt] = 2.0 * (back[j * 64:(j + 1) * 64] - un[j * 2 + xt, src])

    a_core.wait_recv()
    a_mine[...] = ay[0, :, pl.ds(mine, 64)]
    for o in range(8):
        here = pl.ds(o * 8, 8)
        za_out[o] = jnp.where(swap, a0x[:, here], a_mine[:, here])
    za_in[zc] = za_out[zc]
    za = [go(za_out.at[lax.rem(zc + i, RING)], za_in.at[zc], s_ring.at[3, i], r_ring.at[3, i],
             ring_dev(i)) for i in FAR]

    solve_x(0, d_send)
    d_core = go(d_send, d_other, s_core.at[1], r_core.at[1], partner)

    for o in range(8):
        a, h = za_out[o], zm_out[o, 1]
        inv = 1.0 / (zm_out[o, 0] + a + h)
        ym_0[o, 0], ym_0[o, 1], ym_0[o, 2] = inv, a * inv, h * inv
    solve_x(1, d_mine)
    d_core.wait_recv()
    for o in range(8):
        part = pl.ds(o * 8, 8)
        own, far = [d_mine[j, :, part] for j in range(2)], [d_other[j, :, part] for j in range(2)]
        f = ([jnp.where(swap, far[j], own[j]) for j in range(2)]
             + [jnp.where(swap, own[j], far[j]) for j in range(2)])
        g, acc = f[1], f[0]
        for t in range(2):
            y_g[o, t] = g * ym_i[o, t]
            acc = acc + ym_h[o, t] * g
            g = f[t + 2] + ym_r[o, t] * g
        y_g[o, 2] = acc * ym_0[o, 0]
        zr_out[o, 0], zr_out[o, 1] = g + ym_0[o, 2] * acc, ym_0[o, 1] * acc
    zr_in[zc] = zr_out[zc]
    zrc = [go(zr_out.at[lax.rem(zc + i, RING)], zr_in.at[zc], s_ring.at[1, i], r_ring.at[1, i],
              ring_dev(i)) for i in FAR]

    for c in zm + za:
        c.wait_recv()
    chips = []
    for s in range(8):
        low, h, high, a = zm_in[s, 0], zm_in[s, 1], zm_in[s, 2], za_in[s]
        inv = 1.0 / (low + a + h)
        up, down = h * inv, a * inv
        chips.append((high + up * low, down * low, down * h))
    masses = [chips[s][0] + chips[s + 1][1] for s in range(7)] + [chips[7][0]]
    p, h, sigma, ratios, inverses, reach = forward_matrix(
        masses, [c[2] for c in chips])
    yk_out[0], yk_out[1], yk_out[2] = p, chips[0][1] + sigma, h
    for t in range(7):
        l_r[t], l_i[t], l_h[t] = ratios[t], inverses[t], reach[t]
    yk_in[yc] = yk_out[...]
    yk = [go(yk_out, yk_in.at[yc], s_col.at[0, i], r_col.at[0, i], col_dev(i)) for i in FAR]

    for c in zrc:
        c.wait_recv()
    g, acc = zr_in[0, 0] + zr_in[1, 1], None
    for s in range(7):
        l_g[s] = g * l_i[s]
        add = l_h[s] * g
        acc = add if acc is None else acc + add
        g = zr_in[s + 1, 0] + l_r[s] * g
        if s < 6:
            g = g + zr_in[s + 2, 1]
    yr_out[0], yr_out[1] = g, zr_in[0, 1] + acc
    yr_in[yc] = yr_out[...]
    yr = [go(yr_out, yr_in.at[yc], s_col.at[1, i], r_col.at[1, i], col_dev(i)) for i in FAR]

    for c in yk:
        c.wait_recv()
    masses = [yk_in[s, 0] + yk_in[s + 1, 1] for s in range(7)] + [yk_in[7, 0]]
    sub = [yk_in[s, 2] for s in range(8)]
    p, ratios, inverses = masses[0], [], []
    for s in range(1, 8):
        inv = 1.0 / (p + sub[s])
        ratios.append(sub[s] * inv)
        inverses.append(inv)
        p = masses[s] + ratios[-1] * p
    inverses.append(1.0 / p)
    for c in yr:
        c.wait_recv()
    values = [yr_in[0, 0] + yr_in[1, 1]]
    for s in range(1, 8):
        g = yr_in[s, 0] + ratios[s - 1] * values[-1]
        values.append(g + yr_in[s + 1, 1] if s < 7 else g)
    value = values[7] * inverses[7]
    sol8[8] = value
    for s in range(6, -1, -1):
        value = values[s] * inverses[s] + ratios[s] * value
        sol8[s + 1] = value
    sol8[0] = jnp.zeros_like(value)
    left, value = sol8[yc], sol8[yc + 1]
    back_out[7, 1] = value
    for s in range(6, -1, -1):
        value = l_g[s] + l_h[s] * left + l_r[s] * value
        back_out[s, 1] = value
        back_out[s + 1, 0] = value
    back_out[0, 0] = left
    back_in[zc] = back_out[zc]
    bk = [go(back_out.at[lax.rem(zc + i, RING)], back_in.at[zc], s_ring.at[2, i], r_ring.at[2, i],
             ring_dev(i)) for i in FAR]
    for c in bk:
        c.wait_recv()
    for o in range(8):
        part = pl.ds(o * 8, 8)
        left, value = back_in[o, 0], back_in[o, 1]
        start = y_g[o, 2] + ym_0[o, 1] * left + ym_0[o, 2] * value
        third = y_g[o, 1] + ym_h[o, 1] * start + ym_r[o, 1] * value
        solved = [start, y_g[o, 0] + ym_h[o, 0] * start + ym_r[o, 0] * third, third, value]
        for j in range(2):
            back_core[pl.ds(2 * j, 2), part] = jnp.where(swap, solved[j], solved[2 + j])
            d_back[pl.ds(2 * j, 2), part] = jnp.where(swap, solved[2 + j], solved[j])
    home = go(back_core, home_core, s_core.at[2], r_core.at[2], partner)
    zd[:, pl.ds(mine, 64)] = d_back[...]
    home.wait_recv()
    zd[:, pl.ds(other, 64)] = home_core[...]

    g = acc = None
    for t in range(TZ):
        f = zrow(zd, t)
        g = f if t == 0 else f + zr[t] * g
        if t < TZ - 1:
            acc = zh[t] * g if acc is None else acc + zh[t] * g
            zi[t] = g * zi[t]
    g = g + jnp.where(last, 0.0, pltpu.roll(acc, 7, 0))
    levels = [(zlev[2 * i], zlev[2 * i + 1]) for i in range(3)]
    base = spread_solve(levels, zlev[6], jnp.where(last, 0.0, g))
    h = zlev[9]
    nr_own[0] = pick(g, 7) + pick(h, 7) * pick(base, 6)
    nr_own[1] = pick(acc, 0) + pick(h, 0) * pick(base, 0)
    compact(nr_own, nr_out, 2)
    nr = [go(nr_out, nr_in.at[i - 1], s_n.at[1, i], r_n.at[1, i], n_dev(i))
          for i in (2, 1, 3)]
    for c in nm:
        c.wait_recv()

    def stacked(own, ref, v):
        whole = jnp.where(sub8 == n, own, 0.0)
        for i in range(1, 4):
            row = jnp.concatenate(
                [jnp.broadcast_to(ref[i - 1, pl.ds(4 * v + c, 1), :], (8, 128))
                 for c in range(4)], axis=1)
            whole = jnp.where(sub8 == lax.rem(n + 4 - i, 4), row, whole)
        return whole

    top_mass, low_mass, coupling = [stacked(nm_own[v], nm_in, v) for v in range(3)]
    high = pltpu.roll(coupling, 7, 0)
    mass = top_mass + jnp.where(sub8 < 3, pltpu.roll(low_mass, 7, 0), 0.0)
    mass = jnp.where(sub8 < 4, mass, 1.0)
    n_levels, n_inverse = spread_factor(mass, coupling)
    for c in nr:
        c.wait_recv()
    top_rhs, low_rhs = [stacked(nr_own[v], nr_in, v) for v in range(2)]
    rhs = top_rhs + jnp.where(sub8 < 3, pltpu.roll(low_rhs, 7, 0), 0.0)
    ends = spread_solve(n_levels, n_inverse, rhs)
    mine_end = jnp.sum(jnp.where(sub8 == n, ends, 0.0), axis=0, keepdims=True)
    left_end = jnp.sum(jnp.where(sub8 == n - 1, ends, 0.0), axis=0, keepdims=True)
    sep = jnp.where(last, mine_end, base + zlev[7] * left_end + zlev[8] * mine_end)
    left = jnp.where(first, left_end, pltpu.roll(sep, 1, 0))
    value = sep
    for t in range(TZ - 1, -1, -1):
        if t < TZ - 1:
            value = zi[t] + zh[t] * left + zr[t + 1] * value
        for c in range(4):
            zg[c, pl.ds(t, 8, stride=TZ), :] = value[:, c * 128:(c + 1) * 128]
    for j in range(2):
        for xt in range(2):
            c = j * 2 + xt
            out[pl.ds(xt * 2 + j, PLANES, stride=4), :] = un[c, rows] + zg[c]
    for c in pending:
        c.wait_send()


def flat(value):
    return value.reshape(PLANES, 2, 2, 128).transpose(0, 2, 1, 3).reshape(4 * PLANES, 128)


def per_device(initial_heat_level, heat_transmission):
    f32 = jnp.float32
    V = lambda *shape: pltpu.VMEM(shape, f32)
    S = lambda *shape: pltpu.SemaphoreType.DMA(shape)
    natural = (4, PLANES + 2 * PAD, 128)
    halo = (2, PLANES, 128)
    half = (2, 2, 64, 128)
    tile = (2, 8, 128)
    scratch = [
        V(4 * PLANES, 128), V(4 * PLANES, 128), S(2),
        V(*natural), V(*natural), V(*natural),
        V(*halo), V(*halo), V(2, *halo), V(2, 64, 128), V(2, 64, 128),
        V(4, 64, 128), V(2, 64, 128), V(2, 64, 128), V(4, 64, 128), V(3, *halo),
        V(2, X, 128), V(TX, 8, 256), V(TX, 8, 256), V(TX, 8, 256), V(TX, 8, 128),
        V(TZ, 8, 512), V(TZ, 8, 512), V(TZ, 8, 512), V(4, PLANES, 128),
        V(*half), V(*half), V(*half),
        V(8, 3, *tile), V(8, 3, *tile), V(8, 3, *tile), V(8, 3, *tile), V(8, 3, *tile),
        V(8, 3, *tile), V(8, 3, *tile), V(8, *tile), V(8, *tile), V(8, 2, *tile), V(8, 2, *tile),
        V(7, *tile), V(7, *tile), V(7, *tile), V(7, *tile),
        V(3, *tile), V(8, 3, *tile), V(2, *tile), V(8, 2, *tile), V(9, *tile),
        V(8, 2, *tile), V(8, 2, *tile), V(4, 64, 128), V(4, 64, 128), V(4, PLANES, 128),
        V(3, 8, 512), V(16, 128), V(3, 16, 128), V(2, 8, 512), V(8, 128), V(3, 8, 128), V(4, 4, 8, 128),
        V(7, 8, 256), V(10, 8, 512),
        S(6), S(6), S(4), S(4), S(4), S(4), S(4, 8), S(4, 8), S(2, 8), S(2, 8), S(2, 4), S(2, 4),
    ]
    vmem = pl.BlockSpec(memory_space=pltpu.VMEM)
    hbm = pl.BlockSpec(memory_space=pltpu.HBM)
    result = pl.pallas_call(
        kernel,
        out_shape=jax.ShapeDtypeStruct((4 * PLANES, 128), f32),
        in_specs=[hbm, hbm],
        out_specs=vmem,
        scratch_shapes=scratch,
        compiler_params=pltpu.CompilerParams(
            collective_id=0, has_side_effects=True, vmem_limit_bytes=40 << 20),
    )(*[pltpu.with_memory_space_constraint(flat(v), pltpu.HBM)
        for v in (initial_heat_level, heat_transmission)])
    return result.reshape(PLANES, 2, 2, 128).transpose(0, 2, 1, 3).reshape(PLANES, 2, X)


def solution(mesh):
    spec = P("narrow", "wide", None)
    return jax.shard_map(
        per_device, mesh=mesh, in_specs=(spec, spec), out_specs=spec, check_vma=False)
```

```python
import functools

import jax
import jax.numpy as jnp
from jax import lax
from jax.experimental import pallas as pl
from jax.experimental.pallas import tpu as pltpu
from jax.sharding import PartitionSpec as P

MESH = pl.DeviceIdType.MESH
WIDE, RING, PLANES, X = 128, 8, 128, 256
PAD = 8
TX, TZ = 32, 16
FACE = 500.0
FAR = (4, 3, 5, 2, 6, 1, 7)


def face(lower, upper):
    return FACE * lower * upper / (lower + upper)


def forward_matrix(masses, sub):
    p, h = masses[0], sub[0]
    ratios, inverses, reach, sigma = [], [], [], None
    for t in range(1, len(sub)):
        inv = 1.0 / (p + h + sub[t])
        hm = h * inv
        sigma = hm * p if sigma is None else sigma + hm * p
        r = sub[t] * inv
        ratios.append(r)
        inverses.append(inv)
        reach.append(hm)
        p = masses[t] + r * p
        h = r * h
    return p, h, sigma, ratios, inverses, reach


def neighbours(value, step):
    size = value.shape[0]
    return pltpu.roll(value, step, 0), pltpu.roll(value, size - step, 0)


def spread_factor(mass, low):
    high = pltpu.roll(low, 7, 0)
    levels = []
    for step in (1, 2, 4):
        inv = 1.0 / (mass + low + high)
        inv_down, inv_up = neighbours(inv, step)
        alpha, gamma = low * inv_down, high * inv_up
        mass_down, mass_up = neighbours(mass, step)
        mass = mass + alpha * mass_down + gamma * mass_up
        low = alpha * pltpu.roll(low, step, 0)
        high = gamma * pltpu.roll(high, 8 - step, 0)
        levels.append((alpha, gamma))
    return levels, 1.0 / mass


def spread_solve(levels, inverse, value):
    for (alpha, gamma), step in zip(levels, (1, 2, 4)):
        down, up = neighbours(value, step)
        value = value + alpha * down + gamma * up
    return value * inverse


def kernel(u_hbm, k_hbm, out, u_in, k_in, s_load, un, kn, az, uprev, unext, khalo, kx, a0x, k_mine, k_inner, a_mine, d_back, ay,
           work, xr, xi, xh, xg, zr, zi, zh, zg,
           d_send, d_mine, d_other, ym_r, ym_i, ym_h, ym_0, y_g,
           zm_out, zm_in, za_out, za_in, zr_out, zr_in, l_r, l_i, l_h, l_g,
           yk_out, yk_in, yr_out, yr_in, sol8, back_out, back_in, back_core, home_core, zd,
           nm_own, nm_out, nm_in, nr_own, nr_out, nr_in, edge_in, xlev, zlev,
           s_halo, r_halo, s_edge, r_edge, s_core, r_core, s_ring, r_ring, s_col, r_col, s_n, r_n):
    w = lax.axis_index("wide")
    n = lax.axis_index("narrow")
    core = lax.rem(w, 2)
    zc = lax.rem(w // 2, RING)
    yc = w // (2 * RING)
    partner = {"wide": w + 1 - 2 * core}
    upper_dev = {"wide": lax.rem(w + 1, WIDE)}
    lower_dev = {"wide": lax.rem(w + WIDE - 1, WIDE)}

    turned = [i + core * (8 - 2 * i) for i in range(8)]

    def ring_dev(i):
        return {"wide": yc * (2 * RING) + lax.rem(zc + turned[i], RING) * 2 + core}

    def col_dev(i):
        return {"wide": lax.rem(yc + turned[i], RING) * (2 * RING) + zc * 2 + core}

    def n_dev(i):
        return {"narrow": lax.rem(n + i, 4)}

    def copy(src, dst, send, recv, dev):
        return pltpu.make_async_remote_copy(
            src_ref=src, dst_ref=dst, send_sem=send, recv_sem=recv,
            device_id=dev, device_id_type=MESH)

    loads = [pltpu.make_async_copy(k_hbm, k_in, s_load.at[0]),
             pltpu.make_async_copy(u_hbm, u_in, s_load.at[1])]
    for c in loads:
        c.start()
    barrier = pltpu.get_barrier_semaphore()
    for dev in ([upper_dev, lower_dev] + [ring_dev(i) for i in range(1, 8)]
                + [col_dev(i) for i in range(1, 8)] + [n_dev(i) for i in range(1, 4)]):
        pl.semaphore_signal(barrier, 1, device_id=dev, device_id_type=MESH)

    rows = pl.ds(PAD, PLANES)
    for c, src, dst in zip(loads, (k_in, u_in), (kn, un)):
        c.wait()
        for j in range(2):
            for xt in range(2):
                dst[j * 2 + xt, rows] = src[pl.ds(xt * 2 + j, PLANES, stride=4), :]
    row0, row1 = pl.ds(0, 2), pl.ds(2, 2)

    pl.semaphore_wait(barrier, 19)
    pending = []

    def go(src, dst, send, recv, dev):
        c = copy(src, dst, send, recv, dev)
        c.start()
        pending.append(c)
        return c

    mine = pl.multiple_of(core * 64, 64)
    other = pl.multiple_of(64 - core * 64, 64)
    halves = (other, mine)
    outer = go(kn.at[pl.ds(2 * core, 2), pl.ds(pl.multiple_of(PAD + other, 8), 64)], kx,
               s_core.at[0], r_core.at[0], partner)
    k_halo = [go(kn.at[row1, rows], khalo.at[0], s_halo.at[0], r_halo.at[0], upper_dev),
              go(kn.at[row0, rows], khalo.at[1], s_halo.at[1], r_halo.at[1], lower_dev)]
    top, bottom = pl.ds(PAD + PLANES - 8, 8), pl.ds(PAD, 8)
    edge = [go(kn.at[:, top], edge_in.at[0], s_edge.at[0], r_edge.at[0], n_dev(1)),
            go(kn.at[:, bottom], edge_in.at[1], s_edge.at[1], r_edge.at[1], n_dev(3)),
            go(un.at[:, top], edge_in.at[2], s_edge.at[2], r_edge.at[2], n_dev(1)),
            go(un.at[:, bottom], edge_in.at[3], s_edge.at[3], r_edge.at[3], n_dev(3))]
    u_halo = []
    for i, half in enumerate((mine, other)):
        src = pl.ds(pl.multiple_of(PAD + half, 8), 64)
        u_halo.append([
            go(un.at[row1, src], uprev.at[:, pl.ds(half, 64)], s_halo.at[2 + 2 * i],
               r_halo.at[2 + 2 * i], upper_dev),
            go(un.at[row0, src], unext.at[:, pl.ds(half, 64)], s_halo.at[3 + 2 * i],
               r_halo.at[3 + 2 * i], lower_dev)])

    sub8 = lax.broadcasted_iota(jnp.int32, (8, 1), 0)
    first = sub8 == 0

    def to_x(half, block):
        for xt in range(2):
            work[half, pl.ds(xt * 128, 128)] = jnp.concatenate(
                [block(j, xt) for j in range(2)], axis=0).T

    for half in range(2):
        part = pl.ds(pl.multiple_of(PAD + halves[half], 8), 64)
        to_x(half, lambda j, xt: kn[j * 2 + xt, part])

    def xrow(ref, t):
        return jnp.concatenate(
            [ref[c, pl.ds(t, 8, stride=TX), :] for c in range(2)], axis=1)

    k_before = pltpu.roll(xrow(work, TX - 1), 1, 0)
    p = h = sigma = None
    for t in range(TX):
        k_now = xrow(work, t)
        a = face(k_before, k_now)
        k_before = k_now
        if t == 0:
            a = jnp.where(first, 0.0, a)
            p, h = jnp.ones_like(a), a
        else:
            inv = 1.0 / (p + h + a)
            hm = h * inv
            sigma = hm * p if sigma is None else sigma + hm * p
            r = a * inv
            xr[t] = r
            xi[t - 1] = inv
            xh[t - 1] = hm
            p = 1.0 + r * p
            h = r * h
    x_levels, x_inv = spread_factor(p + jnp.where(sub8 == 7, 0.0, pltpu.roll(sigma, 7, 0)), h)
    for i, (alpha, gamma) in enumerate(x_levels):
        xlev[2 * i] = alpha
        xlev[2 * i + 1] = gamma
    xlev[6] = x_inv

    for c in edge:
        c.wait_recv()
    kn[:, pl.ds(0, PAD)] = edge_in[0]
    kn[:, pl.ds(PAD + PLANES, PAD)] = edge_in[1]
    un[:, pl.ds(0, PAD)] = edge_in[2]
    un[:, pl.ds(PAD + PLANES, PAD)] = edge_in[3]
    for q in range(9):
        size = 8 if q == 8 else 16
        low = kn[:, pl.ds(PAD - 1 + q * 16, size)]
        high = kn[:, pl.ds(PAD + q * 16, size)]
        value = face(low, high)
        if q in (0, 8):
            at = lax.broadcasted_iota(jnp.int32, (size, 1), 0)
            value = jnp.where((at == 0) & (n == (0 if q == 0 else 3)), 0.0, value)
        az[:, pl.ds(PAD + q * 16, size)] = value

    swap = core == 1
    outer.wait_recv()
    pltpu.make_async_copy(khalo.at[0], khalo.at[0], r_halo.at[1 - core]).wait()
    k_mine[...] = kn[:, pl.ds(pl.multiple_of(PAD + mine, 8), 64)]
    k_inner[...] = khalo[1 - core, :, pl.ds(mine, 64)]
    for o in range(8):
        here = pl.ds(o * 8, 8)
        own = [k_mine[pl.ds(2 * j, 2), here] for j in range(2)]
        inner = k_inner[:, here]
        outside = kx[:, here]
        cells = [jnp.where(swap, outside, own[0]), jnp.where(swap, inner, own[1]),
                 jnp.where(swap, own[0], inner), jnp.where(swap, own[1], outside)]
        one = jnp.ones_like(inner)
        p, h, sigma, ratios, inverses, reach = forward_matrix(
            [one] * 3, [face(cells[t], cells[t + 1]) for t in range(3)])
        zm_out[o, 0], zm_out[o, 1], zm_out[o, 2] = 1.0 + sigma, h, p
        for t in range(2):
            ym_r[o, t], ym_i[o, t], ym_h[o, t] = ratios[t], inverses[t], reach[t]
    zm_in[zc] = zm_out[zc]
    zm = [go(zm_out.at[lax.rem(zc + turned[i], RING)], zm_in.at[zc], s_ring.at[0, i], r_ring.at[0, i],
             ring_dev(i)) for i in FAR]

    for q in range(8):
        part, src = pl.ds(q * 16, 16), pl.ds(PAD + q * 16, 16)
        mid = face(kn[row0, src], kn[row1, src])
        ay[1, :, part] = mid
        flux = mid * (un[row1, src] - un[row0, src])
        for row, flow in ((row0, flux), (row1, -flux)):
            u = un[row, src]
            up, down = pl.ds(PAD + q * 16 + 1, 16), pl.ds(PAD + q * 16 - 1, 16)
            lz = az[row, up] * (un[row, up] - u) - az[row, src] * (u - un[row, down])
            zg[row, part] = u + lz + flow

    p = h = sigma = None
    def zrow(ref, t):
        return jnp.concatenate([ref[c, pl.ds(t, 8, stride=TZ), :] for c in range(4)], axis=1)

    for t in range(TZ):
        a = zrow(az, PAD + t)
        if t == 0:
            p, h = jnp.ones_like(a), a
        else:
            inv = 1.0 / (p + h + a)
            hm = h * inv
            sigma = hm * p if sigma is None else sigma + hm * p
            r = a * inv
            zr[t] = r
            zi[t - 1] = inv
            zh[t - 1] = hm
            p = 1.0 + r * p
            h = r * h
    last = sub8 == 7
    mass = p + jnp.where(last, 0.0, pltpu.roll(sigma, 7, 0))
    h_up = pltpu.roll(h, 7, 0)
    low = jnp.where(first | last, 0.0, h)
    ground = mass + jnp.where(first, h, 0.0) + jnp.where(sub8 == 6, h_up, 0.0)
    levels, inverse = spread_factor(jnp.where(last, 1.0, ground), low)
    for i, (alpha, gamma) in enumerate(levels):
        zlev[2 * i] = alpha
        zlev[2 * i + 1] = gamma
    zlev[6] = inverse
    from_low = spread_solve(levels, inverse, jnp.where(first, h, 0.0))
    from_high = spread_solve(levels, inverse, jnp.where(sub8 == 6, h_up, 0.0))
    own_mass = spread_solve(levels, inverse, jnp.where(last, 0.0, mass))
    zlev[7] = from_low
    zlev[8] = from_high
    zlev[9] = h

    def pick(value, s):
        return jnp.broadcast_to(value[s:s + 1], value.shape)

    h0, h7 = pick(h, 0), pick(h, 7)
    nm_own[0] = pick(mass, 7) + h7 * pick(own_mass, 6)
    nm_own[1] = pick(sigma, 0) + h0 * pick(own_mass, 0)
    nm_own[2] = h0 * pick(from_high, 0)

    def compact(own, target, count):
        for v in range(count):
            for c in range(4):
                target[pl.ds(4 * v + c, 1), :] = own[v, pl.ds(0, 1), pl.ds(c * 128, 128)]

    nm_out[pl.ds(8, 8), :] = jnp.zeros((8, 128), jnp.float32)
    compact(nm_own, nm_out, 3)
    nm = [go(nm_out, nm_in.at[i - 1], s_n.at[0, i], r_n.at[0, i], n_dev(i))
          for i in (2, 1, 3)]

    pltpu.make_async_copy(khalo.at[0], khalo.at[0], r_halo.at[core]).wait()
    for q in range(8):
        part, src = pl.ds(q * 16, 16), pl.ds(PAD + q * 16, 16)
        ay[0, :, part] = jnp.where(w > 0, face(khalo[0, :, part], kn[row0, src]), 0.0)
    a_core = go(ay.at[0, :, pl.ds(other, 64)], a0x, s_core.at[3], r_core.at[3], partner)
    for q in range(8):
        part, src = pl.ds(q * 16, 16), pl.ds(PAD + q * 16, 16)
        ay[2, :, part] = jnp.where(w < WIDE - 1, face(kn[row1, src], khalo[1, :, part]), 0.0)

    def solve_x(half, target):
        at = halves[half]
        src = pl.ds(pl.multiple_of(PAD + at, 8), 64)
        part = pl.ds(at, 64)
        for c in u_halo[half]:
            c.wait_recv()

        def rhs(j, xt):
            if j == 0:
                return zg[xt, part] - ay[0, xt, part] * (un[xt, src] - uprev[xt, part])
            return zg[2 + xt, part] + ay[2, xt, part] * (unext[xt, part] - un[2 + xt, src])

        to_x(half, rhs)
        lane = pl.ds(half * 128, 128)
        g = acc = None
        for t in range(TX):
            f = work[half, pl.ds(t, 8, stride=TX), :]
            g = f if t == 0 else f + xr[t, :, lane] * g
            if t < TX - 1:
                acc = xh[t, :, lane] * g if acc is None else acc + xh[t, :, lane] * g
                xg[t] = g * xi[t, :, lane]
        g = g + jnp.where(sub8 == 7, 0.0, pltpu.roll(acc, 7, 0))
        sep = spread_solve([(xlev[2 * i, :, lane], xlev[2 * i + 1, :, lane]) for i in range(3)],
                           xlev[6, :, lane], g)
        left = jnp.where(first, 0.0, pltpu.roll(sep, 1, 0))
        value = sep
        for t in range(TX - 1, -1, -1):
            if t < TX - 1:
                value = xg[t] + xh[t, :, lane] * left + xr[t + 1, :, lane] * value
            work[half, pl.ds(t, 8, stride=TX), :] = value
        for xt in range(2):
            back = work[half, pl.ds(xt * 128, 128)].T
            for j in range(2):
                target[j, xt] = 2.0 * (back[j * 64:(j + 1) * 64] - un[j * 2 + xt, src])

    a_core.wait_recv()
    a_mine[...] = ay[0, :, pl.ds(mine, 64)]
    for o in range(8):
        here = pl.ds(o * 8, 8)
        za_out[o] = jnp.where(swap, a0x[:, here], a_mine[:, here])
    za_in[zc] = za_out[zc]
    za = [go(za_out.at[lax.rem(zc + turned[i], RING)], za_in.at[zc], s_ring.at[3, i], r_ring.at[3, i],
             ring_dev(i)) for i in FAR]

    solve_x(0, d_send)
    d_core = go(d_send, d_other, s_core.at[1], r_core.at[1], partner)

    for o in range(8):
        a, h = za_out[o], zm_out[o, 1]
        inv = 1.0 / (zm_out[o, 0] + a + h)
        ym_0[o, 0], ym_0[o, 1], ym_0[o, 2] = inv, a * inv, h * inv
    solve_x(1, d_mine)
    d_core.wait_recv()
    for o in range(8):
        part = pl.ds(o * 8, 8)
        own, far = [d_mine[j, :, part] for j in range(2)], [d_other[j, :, part] for j in range(2)]
        f = ([jnp.where(swap, far[j], own[j]) for j in range(2)]
             + [jnp.where(swap, own[j], far[j]) for j in range(2)])
        g, acc = f[1], f[0]
        for t in range(2):
            y_g[o, t] = g * ym_i[o, t]
            acc = acc + ym_h[o, t] * g
            g = f[t + 2] + ym_r[o, t] * g
        y_g[o, 2] = acc * ym_0[o, 0]
        zr_out[o, 0], zr_out[o, 1] = g + ym_0[o, 2] * acc, ym_0[o, 1] * acc
    zr_in[zc] = zr_out[zc]
    zrc = [go(zr_out.at[lax.rem(zc + turned[i], RING)], zr_in.at[zc], s_ring.at[1, i], r_ring.at[1, i],
              ring_dev(i)) for i in FAR]

    for c in zm + za:
        c.wait_recv()
    chips = []
    for s in range(8):
        low, h, high, a = zm_in[s, 0], zm_in[s, 1], zm_in[s, 2], za_in[s]
        inv = 1.0 / (low + a + h)
        up, down = h * inv, a * inv
        chips.append((high + up * low, down * low, down * h))
    masses = [chips[s][0] + chips[s + 1][1] for s in range(7)] + [chips[7][0]]
    p, h, sigma, ratios, inverses, reach = forward_matrix(
        masses, [c[2] for c in chips])
    yk_out[0], yk_out[1], yk_out[2] = p, chips[0][1] + sigma, h
    for t in range(7):
        l_r[t], l_i[t], l_h[t] = ratios[t], inverses[t], reach[t]
    yk_in[yc] = yk_out[...]
    yk = [go(yk_out, yk_in.at[yc], s_col.at[0, i], r_col.at[0, i], col_dev(i)) for i in FAR]

    for c in zrc:
        c.wait_recv()
    g, acc = zr_in[0, 0] + zr_in[1, 1], None
    for s in range(7):
        l_g[s] = g * l_i[s]
        add = l_h[s] * g
        acc = add if acc is None else acc + add
        g = zr_in[s + 1, 0] + l_r[s] * g
        if s < 6:
            g = g + zr_in[s + 2, 1]
    yr_out[0], yr_out[1] = g, zr_in[0, 1] + acc
    yr_in[yc] = yr_out[...]
    yr = [go(yr_out, yr_in.at[yc], s_col.at[1, i], r_col.at[1, i], col_dev(i)) for i in FAR]

    for c in yk:
        c.wait_recv()
    masses = [yk_in[s, 0] + yk_in[s + 1, 1] for s in range(7)] + [yk_in[7, 0]]
    sub = [yk_in[s, 2] for s in range(8)]
    p, ratios, inverses = masses[0], [], []
    for s in range(1, 8):
        inv = 1.0 / (p + sub[s])
        ratios.append(sub[s] * inv)
        inverses.append(inv)
        p = masses[s] + ratios[-1] * p
    inverses.append(1.0 / p)
    for c in yr:
        c.wait_recv()
    values = [yr_in[0, 0] + yr_in[1, 1]]
    for s in range(1, 8):
        g = yr_in[s, 0] + ratios[s - 1] * values[-1]
        values.append(g + yr_in[s + 1, 1] if s < 7 else g)
    value = values[7] * inverses[7]
    sol8[8] = value
    for s in range(6, -1, -1):
        value = values[s] * inverses[s] + ratios[s] * value
        sol8[s + 1] = value
    sol8[0] = jnp.zeros_like(value)
    left, value = sol8[yc], sol8[yc + 1]
    back_out[7, 1] = value
    for s in range(6, -1, -1):
        value = l_g[s] + l_h[s] * left + l_r[s] * value
        back_out[s, 1] = value
        back_out[s + 1, 0] = value
    back_out[0, 0] = left
    back_in[zc] = back_out[zc]
    bk = [go(back_out.at[lax.rem(zc + turned[i], RING)], back_in.at[zc], s_ring.at[2, i], r_ring.at[2, i],
             ring_dev(i)) for i in FAR]
    for c in bk:
        c.wait_recv()
    home = []
    for o in range(8):
        part = pl.ds(o * 8, 8)
        left, value = back_in[o, 0], back_in[o, 1]
        start = y_g[o, 2] + ym_0[o, 1] * left + ym_0[o, 2] * value
        third = y_g[o, 1] + ym_h[o, 1] * start + ym_r[o, 1] * value
        solved = [start, y_g[o, 0] + ym_h[o, 0] * start + ym_r[o, 0] * third, third, value]
        for j in range(2):
            back_core[pl.ds(2 * j, 2), part] = jnp.where(swap, solved[j], solved[2 + j])
            d_back[pl.ds(2 * j, 2), part] = jnp.where(swap, solved[2 + j], solved[j])
        if o in (3, 7):
            piece = pl.ds((o // 4) * 32, 32)
            home.append(go(back_core.at[:, piece], home_core.at[:, piece], s_core.at[2 + 2 * (o // 4)],
                           r_core.at[2 + 2 * (o // 4)], partner))
    zd[:, pl.ds(mine, 64)] = d_back[...]
    for c in home:
        c.wait_recv()
    zd[:, pl.ds(other, 64)] = home_core[...]

    g = acc = None
    for t in range(TZ):
        f = zrow(zd, t)
        g = f if t == 0 else f + zr[t] * g
        if t < TZ - 1:
            acc = zh[t] * g if acc is None else acc + zh[t] * g
            zi[t] = g * zi[t]
    g = g + jnp.where(last, 0.0, pltpu.roll(acc, 7, 0))
    levels = [(zlev[2 * i], zlev[2 * i + 1]) for i in range(3)]
    base = spread_solve(levels, zlev[6], jnp.where(last, 0.0, g))
    h = zlev[9]
    nr_own[0] = pick(g, 7) + pick(h, 7) * pick(base, 6)
    nr_own[1] = pick(acc, 0) + pick(h, 0) * pick(base, 0)
    compact(nr_own, nr_out, 2)
    nr = [go(nr_out, nr_in.at[i - 1], s_n.at[1, i], r_n.at[1, i], n_dev(i))
          for i in (2, 1, 3)]
    for c in nm:
        c.wait_recv()

    def stacked(own, ref, v):
        whole = jnp.where(sub8 == n, own, 0.0)
        for i in range(1, 4):
            row = jnp.concatenate(
                [jnp.broadcast_to(ref[i - 1, pl.ds(4 * v + c, 1), :], (8, 128))
                 for c in range(4)], axis=1)
            whole = jnp.where(sub8 == lax.rem(n + 4 - i, 4), row, whole)
        return whole

    top_mass, low_mass, coupling = [stacked(nm_own[v], nm_in, v) for v in range(3)]
    high = pltpu.roll(coupling, 7, 0)
    mass = top_mass + jnp.where(sub8 < 3, pltpu.roll(low_mass, 7, 0), 0.0)
    mass = jnp.where(sub8 < 4, mass, 1.0)
    n_levels, n_inverse = spread_factor(mass, coupling)
    for c in nr:
        c.wait_recv()
    top_rhs, low_rhs = [stacked(nr_own[v], nr_in, v) for v in range(2)]
    rhs = top_rhs + jnp.where(sub8 < 3, pltpu.roll(low_rhs, 7, 0), 0.0)
    ends = spread_solve(n_levels, n_inverse, rhs)
    mine_end = jnp.sum(jnp.where(sub8 == n, ends, 0.0), axis=0, keepdims=True)
    left_end = jnp.sum(jnp.where(sub8 == n - 1, ends, 0.0), axis=0, keepdims=True)
    sep = jnp.where(last, mine_end, base + zlev[7] * left_end + zlev[8] * mine_end)
    left = jnp.where(first, left_end, pltpu.roll(sep, 1, 0))
    value = sep
    for t in range(TZ - 1, -1, -1):
        if t < TZ - 1:
            value = zi[t] + zh[t] * left + zr[t + 1] * value
        for c in range(4):
            zg[c, pl.ds(t, 8, stride=TZ), :] = value[:, c * 128:(c + 1) * 128]
    for j in range(2):
        for xt in range(2):
            c = j * 2 + xt
            out[pl.ds(xt * 2 + j, PLANES, stride=4), :] = un[c, rows] + zg[c]
    for c in pending:
        c.wait_send()


def flat(value):
    return value.reshape(PLANES, 2, 2, 128).transpose(0, 2, 1, 3).reshape(4 * PLANES, 128)


def per_device(initial_heat_level, heat_transmission):
    f32 = jnp.float32
    V = lambda *shape: pltpu.VMEM(shape, f32)
    S = lambda *shape: pltpu.SemaphoreType.DMA(shape)
    natural = (4, PLANES + 2 * PAD, 128)
    halo = (2, PLANES, 128)
    half = (2, 2, 64, 128)
    tile = (2, 8, 128)
    scratch = [
        V(4 * PLANES, 128), V(4 * PLANES, 128), S(2),
        V(*natural), V(*natural), V(*natural),
        V(*halo), V(*halo), V(2, *halo), V(2, 64, 128), V(2, 64, 128),
        V(4, 64, 128), V(2, 64, 128), V(2, 64, 128), V(4, 64, 128), V(3, *halo),
        V(2, X, 128), V(TX, 8, 256), V(TX, 8, 256), V(TX, 8, 256), V(TX, 8, 128),
        V(TZ, 8, 512), V(TZ, 8, 512), V(TZ, 8, 512), V(4, PLANES, 128),
        V(*half), V(*half), V(*half),
        V(8, 3, *tile), V(8, 3, *tile), V(8, 3, *tile), V(8, 3, *tile), V(8, 3, *tile),
        V(8, 3, *tile), V(8, 3, *tile), V(8, *tile), V(8, *tile), V(8, 2, *tile), V(8, 2, *tile),
        V(7, *tile), V(7, *tile), V(7, *tile), V(7, *tile),
        V(3, *tile), V(8, 3, *tile), V(2, *tile), V(8, 2, *tile), V(9, *tile),
        V(8, 2, *tile), V(8, 2, *tile), V(4, 64, 128), V(4, 64, 128), V(4, PLANES, 128),
        V(3, 8, 512), V(16, 128), V(3, 16, 128), V(2, 8, 512), V(8, 128), V(3, 8, 128), V(4, 4, 8, 128),
        V(7, 8, 256), V(10, 8, 512),
        S(6), S(6), S(4), S(4), S(5), S(5), S(4, 8), S(4, 8), S(2, 8), S(2, 8), S(2, 4), S(2, 4),
    ]
    vmem = pl.BlockSpec(memory_space=pltpu.VMEM)
    hbm = pl.BlockSpec(memory_space=pltpu.HBM)
    result = pl.pallas_call(
        kernel,
        out_shape=jax.ShapeDtypeStruct((4 * PLANES, 128), f32),
        in_specs=[hbm, hbm],
        out_specs=vmem,
        scratch_shapes=scratch,
        compiler_params=pltpu.CompilerParams(
            collective_id=0, has_side_effects=True, vmem_limit_bytes=40 << 20),
    )(*[pltpu.with_memory_space_constraint(flat(v), pltpu.HBM)
        for v in (initial_heat_level, heat_transmission)])
    return result.reshape(PLANES, 2, 2, 128).transpose(0, 2, 1, 3).reshape(PLANES, 2, X)


def solution(mesh):
    spec = P("narrow", "wide", None)
    return jax.shard_map(
        per_device, mesh=mesh, in_specs=(spec, spec), out_specs=spec, check_vma=False)
```
